256 devices in a mesh: tm: 4 (over z_hi, core), height: 16 (over x, y), width: 4 (over z_lo).
Axes of the slice: x: 4, y: 4, z: 8 (z_hi: 2, z_lo: 4; z = z_hi * 4 + z_lo), core: 2. Of those that a mesh axis runs over, the one named last changes fastest.
Arguments:
- frames: bfloat16 [8, 64, 128, 384], P('tm', 'height', 'width'), may hold values from -6 to 6
- cache_in: bfloat16 [2, 64, 128, 384], P(None, 'height', 'width'), may hold values from -6 to 6
- kernel: bfloat16 [384, 3, 3, 3, 384], replicated, may hold values from -0.0625 to 0.0625
- conv_bias: float32 [384], replicated, may hold values from -3 to 3
- cotangent: bfloat16 [8, 64, 128, 384], P('tm', 'height', 'width'), may hold values from -6 to 6
Outputs:
- decoded: bfloat16 [8, 64, 128, 384], P('tm', 'height', 'width')
- frame_grad: bfloat16 [8, 64, 128, 384], P('tm', 'height', 'width')
- cache_grad: bfloat16 [8, 64, 128, 384], P('tm', 'height', 'width')
- kernel_grad: float32 [384, 3, 3, 3, 384], P('height')
The draws below stay inside these ranges and needn't reach their ends.
All inputs are finite; a program needn't handle non-finite values.
Results may differ from the reference program's by a relative error of at most 0.0053.
Values may be sent and summed in bfloat16 or wider, within the bound.
No kernel may reach another device: no remote copies, remote signals or barrier semaphores. Data moves between devices by JAX's collectives and lax.ppermute only.
A program may use at most 256 MiB of HBM per device.

```python
import jax
import jax.numpy as jnp

C = 384
F_DEV = 2
FRAMES = 8
ROWS = 64
COLS = 128
N_TM = 4


def strengthened(entries, own_key, source, target, parts, factor):
    def block_of(axis_at):
        return (jnp.arange(entries.shape[axis_at]) // (entries.shape[axis_at] // parts)).reshape((-1,) + (1,) * (entries.ndim - 1 - axis_at))

    one_side = jax.random.permutation(own_key, parts)[block_of(target)]
    other_side = (block_of(target) + parts // 2) % parts
    return jnp.where((block_of(source) == one_side) | (block_of(source) == other_side), factor * entries, entries)


def levels(rng, extent, cuts, low, largest):
    factor_of = 1.0
    for dim, parts in cuts:
        heights = jax.random.uniform(jax.random.fold_in(jax.random.fold_in(rng, 6), dim), (parts,), jnp.float32, low / len(cuts), largest / len(cuts))
        factor_of = factor_of * jnp.repeat(jnp.exp(heights), extent[dim] // parts).reshape((-1,) + (1,) * (len(extent) - 1 - dim))
    return factor_of


def noise(key, dims, scale, reach, split=(), held_as=jnp.bfloat16):
    drawn = jax.random.normal(key, dims, jnp.float32) * scale
    if len(split) > 0:
        drawn = levels(key, dims, split, -0.22, 0.18) * drawn
    return jnp.clip(drawn, min=-reach, max=reach).astype(held_as)


def gaussian_with(key, dims, width, limit, cuts, heavy, dtype=jnp.bfloat16):
    drawn = width * jax.random.normal(key, dims, jnp.float32)
    if cuts:
        drawn = drawn * levels(key, dims, cuts, -0.22, 0.18)
    return jnp.clip(strengthened(drawn, jax.random.fold_in(key, 3), *heavy), -limit, limit).astype(dtype)


def setup_inputs(seed: int = 0) -> dict:
    key_of = jax.random.split(jax.random.key(seed), 6)
    frames = noise(key_of[0], (FRAMES, ROWS, COLS, C), 1.0, 6.0, ((0, 4), (1, 16), (2, 4)))
    cache_in = noise(key_of[1], (2, ROWS, COLS, C), 1.0, 6.0, ((1, 16), (2, 4)))
    kernel = noise(key_of[2], (C, 3, 3, 3, C), (27 * C) ** -0.5, 0.0625)
    conv_bias = noise(key_of[3], (C,), 0.5, 3.0, (), jnp.float32)
    cotangent = gaussian_with(key_of[4], (FRAMES, ROWS, COLS, C), 1.0, 6.0, ((0, 4), (1, 16), (2, 4)), (1, 3, 16, 2.0))
    return dict(frames=frames, cache_in=cache_in, kernel=kernel, conv_bias=conv_bias, cotangent=cotangent)


def tap_block(padded, tap_t, tap_h, tap_w, depth_count, row_count, col_count):
    block = padded[tap_t:tap_t + depth_count, tap_h:tap_h + row_count, tap_w:tap_w + col_count]
    return block.reshape(-1, block.shape[-1])


def reference(frames, cache_in, kernel, conv_bias, cotangent):
    frame_count, row_count, col_count, channels = frames.shape
    joined = jnp.concatenate([cache_in, frames], 0)
    padded = jnp.pad(joined, ((0, 0), (1, 1), (1, 1), (0, 0)))
    pre_act = jnp.zeros((frame_count * row_count * col_count, channels), jnp.float32) + conv_bias
    for tap_t in range(3):
        for tap_h in range(3):
            for tap_w in range(3):
                block = tap_block(padded, tap_t, tap_h, tap_w, frame_count, row_count, col_count)
                pre_act = pre_act + jnp.dot(block, kernel[:, tap_t, tap_h, tap_w, :].T, preferred_element_type=jnp.float32)
    sigma = jax.nn.sigmoid(pre_act)
    decoded = (pre_act * sigma).astype(jnp.bfloat16).reshape(frames.shape)
    scaled = (cotangent.reshape(-1, channels).astype(jnp.float32) * sigma * (1.0 + pre_act * (1.0 - sigma))).astype(jnp.bfloat16)
    grad_pad = jnp.pad(scaled.reshape(frames.shape), ((0, 0), (1, 1), (1, 1), (0, 0)))
    partial_value = jnp.zeros((N_TM, F_DEV + 2, row_count, col_count, channels), jnp.float32)
    for tap_t in range(3):
        contrib = jnp.zeros((frame_count * row_count * col_count, channels), jnp.float32)
        for tap_h in range(3):
            for tap_w in range(3):
                block = grad_pad[:, 2 - tap_h:2 - tap_h + row_count, 2 - tap_w:2 - tap_w + col_count].reshape(-1, channels)
                contrib = contrib + jnp.dot(block, kernel[:, tap_t, tap_h, tap_w, :], preferred_element_type=jnp.float32)
        partial_value = partial_value.at[:, tap_t:tap_t + F_DEV].add(contrib.reshape(N_TM, F_DEV, row_count, col_count, channels))
    head = partial_value[:, :2].astype(jnp.bfloat16)
    cache_grad = head.reshape(2 * N_TM, row_count, col_count, channels)
    carried = jnp.concatenate([head[1:], jnp.zeros_like(head[:1])], 0)
    tail = partial_value[:, 2:].at[:, F_DEV - 2:].add(carried.astype(jnp.float32))
    frame_grad = tail.reshape(frames.shape).astype(jnp.bfloat16)
    pieces = []
    for tap_t in range(3):
        for tap_h in range(3):
            for tap_w in range(3):
                block = tap_block(padded, tap_t, tap_h, tap_w, frame_count, row_count, col_count)
                pieces.append(jnp.dot(scaled.T, block, preferred_element_type=jnp.float32))
    kernel_grad = jnp.stack(pieces, 1).reshape(channels, 3, 3, 3, channels)
    return decoded, frame_grad, cache_grad, kernel_grad
```

```python
import jax
import jax.numpy as jnp
from jax import lax
from jax.experimental import pallas as pl
from jax.experimental.pallas import tpu as pltpu
from jax.sharding import Mesh, PartitionSpec as P

BF = jnp.bfloat16
F32 = jnp.float32
TM = ("zh", "co")
HEIGHT = ("x", "y")
RING = ("zh", "z")
STREAM_TAPS = (4, 3, 4, 3)
STREAM_START = (0, 4, 7, 11)
STREAM_ORDER = ((0, 3, 1, 2), (0, 1, 3, 2), (0, 3, 1, 2), (0, 1, 3, 2))
N_TAPS = 14


def shifted(value, axis, by):
    length = lax.axis_size(axis)
    pairs = [(i, i + by) for i in range(length) if 0 <= i + by < length]
    return lax.ppermute(value, axis, pairs)


def exchanged(value, axis, flip):
    return lax.ppermute(value, axis, [(i, i ^ flip) for i in range(lax.axis_size(axis))])


def with_halo(value, sides, width):
    for axis, dim in sides:
        size, length = (lax.axis_size(axis), value.shape[dim])
        up = [(i, (i + 1) % size) for i in range(size - 1)]
        down = [(j, i) for i, j in up]
        last = lax.slice_in_dim(value, length - width, length, axis=dim)
        initial = lax.slice_in_dim(value, 0, width, axis=dim)
        before = lax.ppermute(last, axis, up)
        after = lax.ppermute(initial, axis, down)
        value = jnp.concatenate([before, value, after], axis=dim)
    return value


def tap_block(padded, tap_t, tap_h, tap_w, depth_count, row_count, col_count):
    block = padded[
        tap_t : tap_t + depth_count, tap_h : tap_h + row_count, tap_w : tap_w + col_count
    ]
    return block.reshape(-1, block.shape[-1])


def selectors(channels):
    at_x, at_y = lax.axis_index("x"), lax.axis_index("y")
    row = lax.broadcasted_iota(jnp.int32, (channels, channels), 0)
    col = lax.broadcasted_iota(jnp.int32, (channels, channels), 1)
    outer, inner, rest = row // 96, (row // 24) % 4, row % 24
    out = []
    for stream, order in enumerate(STREAM_ORDER):
        def rel(v):
            return jnp.where(
                v == 0, order[0], jnp.where(v == 1, order[1], jnp.where(v == 2, order[2], order[3]))
            )

        if stream < 2:
            dest_x, dest_y = at_x ^ rel(outer), at_y ^ rel(inner)
        else:
            dest_y, dest_x = at_y ^ rel(outer), at_x ^ rel(inner)
        out.append((dest_x * 96 + dest_y * 24 + rest == col).astype(BF))
    return jnp.stack(out)


def weight_grad_kernel(core_ref, ext_ref, more_ref, own_ref, peer_ref, sel_ref, *rest):
    outs, (cols, lhs) = rest[:8], rest[8:]
    step = pl.program_id(0)
    core = core_ref[0]

    @pl.when(step == 0)
    def _():
        for c in range(3):
            for f in range(4):
                cols[c, f + core] = ext_ref[f, :, c : c + 32, :]
            cols[c, 4 * (1 - core)] = more_ref[:, c : c + 32, :]
        for s in range(4):
            for half, ref in enumerate((own_ref, peer_ref)):
                lhs[s, half] = lax.dot_general(
                    sel_ref[s], ref[...], (((1,), (1,)), ((), ())), preferred_element_type=F32
                ).astype(BF)

    k = step + 4 * core
    tap_t, tap_h, tap_w = k // 9, (k // 3) % 3, k % 3
    mine = cols[tap_w, pl.ds(tap_t + 2 * core, 2), pl.ds(tap_h, 4)].reshape(256, 384)
    theirs = cols[tap_w, pl.ds(tap_t + 2 * (1 - core), 2), pl.ds(tap_h, 4)].reshape(256, 384)
    for s in range(4):
        @pl.when((step >= STREAM_START[s]) & (step < STREAM_START[s] + STREAM_TAPS[s]))
        def _():
            total = jnp.dot(lhs[s, 0], mine, preferred_element_type=F32)
            total = total + jnp.dot(lhs[s, 1], theirs, preferred_element_type=F32)
            outs[2 * s][0] = total[:192].astype(BF)
            outs[2 * s + 1][0] = total[192:].astype(BF)


def weight_grad(core, ext, more, own, peer, sel):
    def whole(a):
        return pl.BlockSpec(a.shape, lambda j, *_: (0,) * a.ndim)

    def part(s):
        return pl.BlockSpec(
            (1, 192, 384),
            lambda j, *_: (jnp.clip(j - STREAM_START[s], 0, STREAM_TAPS[s] - 1), 0, 0),
        )

    shapes, specs = [], []
    for s in range(4):
        shapes += [jax.ShapeDtypeStruct((STREAM_TAPS[s], 192, 384), BF)] * 2
        specs += [part(s)] * 2
    return pl.pallas_call(
        weight_grad_kernel,
        out_shape=shapes,
        grid_spec=pltpu.PrefetchScalarGridSpec(
            num_scalar_prefetch=1,
            grid=(N_TAPS,),
            in_specs=[whole(a) for a in (ext, more, own, peer, sel)],
            out_specs=specs,
            scratch_shapes=[
                pltpu.VMEM((3, 5, 6, 32, 384), BF),
                pltpu.VMEM((4, 2, 384, 256), BF),
            ],
        ),
        compiler_params=pltpu.CompilerParams(vmem_limit_bytes=48 << 20),
        cost_estimate=pl.CostEstimate(
            flops=2 * N_TAPS * 384 * 384 * 512, bytes_accessed=8 << 20, transcendentals=0
        ),
    )(core, ext, more, own, peer, sel)


def halved(keep, sent, axes, flips):
    got = [exchanged(v, a, f) for v, a, f in zip(sent, axes, flips)]
    return [k.astype(F32) + g.astype(F32) for k, g in zip(keep, got)]


def reduced_over_xy(parts):
    keep, sent = list(parts[0::2]), list(parts[1::2])
    total = None
    for axes in (("x", "x", "y", "y"), ("y", "y", "x", "x")):
        for flips in ((1, 3, 1, 3), (3, 1, 3, 1)):
            if total is not None:
                half = [v.shape[1] // 2 for v in total]
                keep = [v[:, :h] for v, h in zip(total, half)]
                sent = [v[:, h:].astype(BF) for v, h in zip(total, half)]
            total = halved(keep, sent, axes, flips)
    return jnp.concatenate(total, 0)


def reduced_over_ring(mine):
    at = lax.axis_index(RING)
    chunks = mine.reshape(7, 2, 24, 384)
    total = lax.dynamic_index_in_dim(chunks, jnp.minimum(at, 6), 0, keepdims=False)
    for k in range(1, 8):
        out = lax.dynamic_index_in_dim(chunks, jnp.minimum((at + k) % 8, 6), 0, keepdims=False)
        pairs = [(i, (i + k) % 8) for i in range(8) if (i + k) % 8 < 7]
        total = total + lax.ppermute(out.astype(BF), RING, pairs).astype(F32)
    total = lax.optimization_barrier(total.astype(BF))
    parts = [total]
    for k in range(1, 8):
        pairs = [(i, (i + k) % 8) for i in range(7)]
        parts.append(lax.ppermute(total, RING, pairs))
    back = jnp.stack([parts[(-i) % 8] for i in range(8)])
    whole = lax.dynamic_slice_in_dim(jnp.concatenate([back, back]), (8 - at) % 8, 7, 0)
    return lax.optimization_barrier(whole.reshape(N_TAPS, 24, 384))


def body(frames, cache_in, kernel, conv_bias, cotangent):
    frame_count, row_count, col_count, channels = frames.shape
    core = lax.axis_index("co")
    is_first = lax.axis_index(TM) == 0
    weights = kernel.transpose(1, 2, 3, 0, 4)
    earlier = shifted(frames, TM, 1)
    earlier = jnp.where(is_first, cache_in, earlier)
    stacked = jnp.concatenate([earlier, frames], 0)
    extended = with_halo(stacked, ((HEIGHT, 1), ("z", 2)), 1)
    more = exchanged(jnp.where(core == 0, extended[1], extended[2]), "co", 1)
    pre_act = jnp.zeros((frame_count * row_count * col_count, channels), F32) + conv_bias
    for tap_t in range(3):
        for tap_h in range(3):
            for tap_w in range(3):
                block = tap_block(extended, tap_t, tap_h, tap_w, frame_count, row_count, col_count)
                pre_act = pre_act + lax.dot_general(
                    block,
                    weights[tap_t, tap_h, tap_w],
                    (((1,), (1,)), ((), ())),
                    preferred_element_type=F32,
                )
    sigma = jax.nn.sigmoid(pre_act)
    decoded = (pre_act * sigma).astype(BF).reshape(frames.shape)
    scaled = (
        cotangent.reshape(-1, channels).astype(F32) * sigma * (1.0 + pre_act * (1.0 - sigma))
    ).astype(BF)
    peer = exchanged(scaled, "co", 1)
    parts = weight_grad(core.reshape(1), extended, more, scaled, peer, selectors(channels))
    mine = reduced_over_ring(reduced_over_xy(parts))
    theirs = exchanged(mine, "co", 1)
    taps = jnp.where(
        core == 0,
        jnp.concatenate([mine, theirs[1:]], 0),
        jnp.concatenate([theirs, mine[1:]], 0),
    ).astype(F32)
    kernel_grad = taps.reshape(3, 3, 3, 24, channels).transpose(3, 0, 1, 2, 4)

    grad_rimmed = with_halo(scaled.reshape(frames.shape), ((HEIGHT, 1), ("z", 2)), 1)
    partial_value = jnp.zeros((frame_count + 2, row_count, col_count, channels), F32)
    for tap_t in range(3):
        contrib = jnp.zeros((frame_count * row_count * col_count, channels), F32)
        for tap_h in range(3):
            for tap_w in range(3):
                block = grad_rimmed[
                    :, 2 - tap_h : 2 - tap_h + row_count, 2 - tap_w : 2 - tap_w + col_count
                ].reshape(-1, channels)
                contrib = contrib + jnp.dot(
                    block, weights[tap_t, tap_h, tap_w], preferred_element_type=F32
                )
        partial_value = partial_value.at[tap_t : tap_t + frame_count].add(
            contrib.reshape(frame_count, row_count, col_count, channels)
        )
    cache_grad = partial_value[:2].astype(BF)
    carried = shifted(cache_grad, TM, -1)
    frame_grad = (
        partial_value[2:].at[frame_count - 2 :].add(carried.astype(F32)).astype(BF)
    )
    return (decoded, frame_grad, cache_grad, kernel_grad)


def solution(mesh):
    split = Mesh(mesh.devices.reshape(2, 2, 4, 4, 4), ("zh", "co", "x", "y", "z"))
    block = P(TM, HEIGHT, "z", None)
    return jax.shard_map(
        body,
        mesh=split,
        in_specs=(block, P(None, HEIGHT, "z", None), P(), P(), block),
        out_specs=(block, block, block, P(HEIGHT, None, None, None, None)),
        check_vma=False,
    )
```

```python
import jax
import jax.numpy as jnp
from jax import lax
from jax.experimental import pallas as pl
from jax.experimental.pallas import tpu as pltpu
from jax.sharding import Mesh, PartitionSpec as P

BF = jnp.bfloat16
F32 = jnp.float32
TM = ("zh", "co")
HEIGHT = ("x", "y")
RING = ("zh", "z")
STREAM_TAPS = (4, 3, 4, 3)
STREAM_START = (0, 4, 7, 11)
STREAM_ORDER = ((0, 3, 1, 2), (0, 1, 3, 2), (0, 3, 1, 2), (0, 1, 3, 2))
N_TAPS = 14


def shifted(value, axis, by):
    length = lax.axis_size(axis)
    pairs = [(i, i + by) for i in range(length) if 0 <= i + by < length]
    return lax.ppermute(value, axis, pairs)


def exchanged(value, axis, flip):
    return lax.ppermute(value, axis, [(i, i ^ flip) for i in range(lax.axis_size(axis))])


def with_halo(value, sides, width):
    for axis, dim in sides:
        size, length = (lax.axis_size(axis), value.shape[dim])
        up = [(i, (i + 1) % size) for i in range(size - 1)]
        down = [(j, i) for i, j in up]
        last = lax.slice_in_dim(value, length - width, length, axis=dim)
        initial = lax.slice_in_dim(value, 0, width, axis=dim)
        before = lax.ppermute(last, axis, up)
        after = lax.ppermute(initial, axis, down)
        value = jnp.concatenate([before, value, after], axis=dim)
    return value


def tap_block(padded, tap_t, tap_h, tap_w, depth_count, row_count, col_count):
    block = padded[
        tap_t : tap_t + depth_count, tap_h : tap_h + row_count, tap_w : tap_w + col_count
    ]
    return block.reshape(-1, block.shape[-1])


def selectors(channels):
    at_x, at_y = lax.axis_index("x"), lax.axis_index("y")
    row = lax.broadcasted_iota(jnp.int32, (channels, channels), 0)
    col = lax.broadcasted_iota(jnp.int32, (channels, channels), 1)
    outer, inner, rest = row // 96, (row // 24) % 4, row % 24
    out = []
    for stream, order in enumerate(STREAM_ORDER):
        def rel(v):
            return jnp.where(
                v == 0, order[0], jnp.where(v == 1, order[1], jnp.where(v == 2, order[2], order[3]))
            )

        if stream < 2:
            dest_x, dest_y = at_x ^ rel(outer), at_y ^ rel(inner)
        else:
            dest_y, dest_x = at_y ^ rel(outer), at_x ^ rel(inner)
        out.append((dest_x * 96 + dest_y * 24 + rest == col).astype(BF))
    return jnp.stack(out)


def weight_grad_kernel(core_ref, ext_ref, more_ref, own_ref, peer_ref, sel_ref, *rest):
    outs, (cols, lhs) = rest[:8], rest[8:]
    step = pl.program_id(0)
    core = core_ref[0]

    @pl.when(step == 0)
    def _():
        for c in range(3):
            for f in range(4):
                cols[c, f + core] = ext_ref[f, :, c : c + 32, :]
            cols[c, 4 * (1 - core)] = more_ref[:, c : c + 32, :]
        for s in range(4):
            for half, ref in enumerate((own_ref, peer_ref)):
                lhs[s, half] = lax.dot_general(
                    sel_ref[s], ref[...], (((1,), (1,)), ((), ())), preferred_element_type=F32
                ).astype(BF)

    k = step + 4 * core
    tap_t, tap_h, tap_w = k // 9, (k // 3) % 3, k % 3
    mine = cols[tap_w, pl.ds(tap_t + 2 * core, 2), pl.ds(tap_h, 4)].reshape(256, 384)
    theirs = cols[tap_w, pl.ds(tap_t + 2 * (1 - core), 2), pl.ds(tap_h, 4)].reshape(256, 384)
    for s in range(4):
        @pl.when((step >= STREAM_START[s]) & (step < STREAM_START[s] + STREAM_TAPS[s]))
        def _():
            total = jnp.dot(lhs[s, 0], mine, preferred_element_type=F32)
            total = total + jnp.dot(lhs[s, 1], theirs, preferred_element_type=F32)
            outs[2 * s][0] = total[:192].astype(BF)
            outs[2 * s + 1][0] = total[192:].astype(BF)


def weight_grad(core, ext, more, own, peer, sel):
    def whole(a):
        return pl.BlockSpec(a.shape, lambda j, *_: (0,) * a.ndim)

    def part(s):
        return pl.BlockSpec(
            (1, 192, 384),
            lambda j, *_: (jnp.clip(j - STREAM_START[s], 0, STREAM_TAPS[s] - 1), 0, 0),
        )

    shapes, specs = [], []
    for s in range(4):
        shapes += [jax.ShapeDtypeStruct((STREAM_TAPS[s], 192, 384), BF)] * 2
        specs += [part(s)] * 2
    return pl.pallas_call(
        weight_grad_kernel,
        out_shape=shapes,
        grid_spec=pltpu.PrefetchScalarGridSpec(
            num_scalar_prefetch=1,
            grid=(N_TAPS,),
            in_specs=[whole(a) for a in (ext, more, own, peer, sel)],
            out_specs=specs,
            scratch_shapes=[
                pltpu.VMEM((3, 5, 6, 32, 384), BF),
                pltpu.VMEM((4, 2, 384, 256), BF),
            ],
        ),
        compiler_params=pltpu.CompilerParams(vmem_limit_bytes=48 << 20),
        cost_estimate=pl.CostEstimate(
            flops=2 * N_TAPS * 384 * 384 * 512, bytes_accessed=8 << 20, transcendentals=0
        ),
    )(core, ext, more, own, peer, sel)


def halved(keep, sent, axes, flips):
    got = [exchanged(v, a, f) for v, a, f in zip(sent, axes, flips)]
    return [k.astype(F32) + g.astype(F32) for k, g in zip(keep, got)]


def reduced_over_xy(parts):
    keep, sent = list(parts[0::2]), list(parts[1::2])
    total = None
    for axes in (("x", "x", "y", "y"), ("y", "y", "x", "x")):
        for flips in ((1, 3, 1, 3), (3, 1, 3, 1)):
            if total is not None:
                half = [v.shape[1] // 2 for v in total]
                keep = [v[:, :h] for v, h in zip(total, half)]
                sent = [v[:, h:].astype(BF) for v, h in zip(total, half)]
            total = halved(keep, sent, axes, flips)
    return jnp.concatenate(total, 0)


def reduced_over_ring(mine):
    chunks = mine.astype(BF).reshape(8, 42, 384)
    got = lax.all_to_all(chunks, RING, 0, 0, tiled=True)
    total = jnp.sum(got.astype(F32), 0).astype(BF)
    whole = lax.all_to_all(jnp.broadcast_to(total, chunks.shape), RING, 0, 0, tiled=True)
    return whole.reshape(N_TAPS, 24, 384)


def body(frames, cache_in, kernel, conv_bias, cotangent):
    frame_count, row_count, col_count, channels = frames.shape
    core = lax.axis_index("co")
    is_first = lax.axis_index(TM) == 0
    weights = kernel.transpose(1, 2, 3, 0, 4)
    earlier = shifted(frames, TM, 1)
    earlier = jnp.where(is_first, cache_in, earlier)
    stacked = jnp.concatenate([earlier, frames], 0)
    extended = with_halo(stacked, ((HEIGHT, 1), ("z", 2)), 1)
    more = exchanged(jnp.where(core == 0, extended[1], extended[2]), "co", 1)
    pre_act = jnp.zeros((frame_count * row_count * col_count, channels), F32) + conv_bias
    for tap_t in range(3):
        for tap_h in range(3):
            if tap_t * 3 + tap_h == 5:
                pre_act, more = lax.optimization_barrier((pre_act, more))
            for tap_w in range(3):
                block = tap_block(extended, tap_t, tap_h, tap_w, frame_count, row_count, col_count)
                pre_act = pre_act + lax.dot_general(
                    block,
                    weights[tap_t, tap_h, tap_w],
                    (((1,), (1,)), ((), ())),
                    preferred_element_type=F32,
                )
    sigma = jax.nn.sigmoid(pre_act)
    decoded = (pre_act * sigma).astype(BF).reshape(frames.shape)
    scaled = (
        cotangent.reshape(-1, channels).astype(F32) * sigma * (1.0 + pre_act * (1.0 - sigma))
    ).astype(BF)
    peer = exchanged(scaled, "co", 1)
    parts = weight_grad(core.reshape(1), extended, more, scaled, peer, selectors(channels))
    scaled, *parts = lax.optimization_barrier((scaled, *parts))
    mine = reduced_over_ring(reduced_over_xy(parts))
    theirs = exchanged(mine, "co", 1)
    taps = jnp.where(
        core == 0,
        jnp.concatenate([mine, theirs[1:]], 0),
        jnp.concatenate([theirs, mine[1:]], 0),
    ).astype(F32)
    kernel_grad = taps.reshape(3, 3, 3, 24, channels).transpose(3, 0, 1, 2, 4)

    grad_rimmed = with_halo(scaled.reshape(frames.shape), ((HEIGHT, 1), ("z", 2)), 1)
    partial_value = jnp.zeros((frame_count + 2, row_count, col_count, channels), F32)
    for tap_t in range(3):
        contrib = jnp.zeros((frame_count * row_count * col_count, channels), F32)
        for tap_h in range(3):
            for tap_w in range(3):
                block = grad_rimmed[
                    :, 2 - tap_h : 2 - tap_h + row_count, 2 - tap_w : 2 - tap_w + col_count
                ].reshape(-1, channels)
                contrib = contrib + jnp.dot(
                    block, weights[tap_t, tap_h, tap_w], preferred_element_type=F32
                )
        partial_value = partial_value.at[tap_t : tap_t + frame_count].add(
            contrib.reshape(frame_count, row_count, col_count, channels)
        )
    cache_grad = partial_value[:2].astype(BF)
    carried = shifted(cache_grad, TM, -1)
    frame_grad = (
        partial_value[2:].at[frame_count - 2 :].add(carried.astype(F32)).astype(BF)
    )
    return (decoded, frame_grad, cache_grad, kernel_grad)


def solution(mesh):
    split = Mesh(mesh.devices.reshape(2, 2, 4, 4, 4), ("zh", "co", "x", "y", "z"))
    block = P(TM, HEIGHT, "z", None)
    return jax.shard_map(
        body,
        mesh=split,
        in_specs=(block, P(None, HEIGHT, "z", None), P(), P(), block),
        out_specs=(block, block, block, P(HEIGHT, None, None, None, None)),
        check_vma=False,
    )
```

```python
import jax
import jax.numpy as jnp
from jax import lax
from jax.experimental import pallas as pl
from jax.experimental.pallas import tpu as pltpu
from jax.sharding import Mesh, PartitionSpec as P

BF = jnp.bfloat16
F32 = jnp.float32
TM = ("zh", "co")
HEIGHT = ("x", "y")
RING = ("zh", "z")
N_TAPS = 14


def shifted(value, axis, by):
    length = lax.axis_size(axis)
    pairs = [(i, i + by) for i in range(length) if 0 <= i + by < length]
    return lax.ppermute(value, axis, pairs)


def exchanged(value, axis, flip):
    return lax.ppermute(value, axis, [(i, i ^ flip) for i in range(lax.axis_size(axis))])


def with_halo(value, sides, width):
    for axis, dim in sides:
        size, length = (lax.axis_size(axis), value.shape[dim])
        up = [(i, (i + 1) % size) for i in range(size - 1)]
        down = [(j, i) for i, j in up]
        last = lax.slice_in_dim(value, length - width, length, axis=dim)
        initial = lax.slice_in_dim(value, 0, width, axis=dim)
        before = lax.ppermute(last, axis, up)
        after = lax.ppermute(initial, axis, down)
        value = jnp.concatenate([before, value, after], axis=dim)
    return value


def tap_block(padded, tap_t, tap_h, tap_w, depth_count, row_count, col_count):
    block = padded[
        tap_t : tap_t + depth_count, tap_h : tap_h + row_count, tap_w : tap_w + col_count
    ]
    return block.reshape(-1, block.shape[-1])


def spread_kernel(where_ref, *refs):
    lines, peer_ref, out_ref = refs[:4], refs[4], refs[5]
    core = where_ref[0]
    for k, flip in enumerate((0, 1, 3, 2)):
        src = where_ref[1] ^ flip
        at = jnp.where(src == 0, 0, 1 + 4 * src)
        for c in range(3):
            for f in range(3):
                out_ref[c, f + 2 * core, pl.ds(at, 5)] = lines[k][f, :, c : c + 32, :]
            for f in range(2):
                out_ref[c, f + 3 * (1 - core), pl.ds(at, 5)] = peer_ref[k, f, :, c : c + 32, :]


def spread(where, lines, peer):
    shape = (3, 5, 18, 32, 384)
    args = (*lines, peer)

    def whole(shape):
        return pl.BlockSpec(shape, lambda i, *_: (0,) * len(shape))

    return pl.pallas_call(
        spread_kernel,
        out_shape=jax.ShapeDtypeStruct(shape, BF),
        grid_spec=pltpu.PrefetchScalarGridSpec(
            num_scalar_prefetch=1,
            grid=(1,),
            in_specs=[whole(a.shape) for a in args],
            out_specs=whole(shape),
        ),
        compiler_params=pltpu.CompilerParams(vmem_limit_bytes=48 << 20),
        cost_estimate=pl.CostEstimate(flops=0, bytes_accessed=12 << 20, transcendentals=0),
    )(where, *args)


def weight_grad_kernel(core_ref, cols, own_ref, peer_ref, out_ref):
    core = core_ref[0]
    k = pl.program_id(0) + 4 * core
    tap_t, tap_h, tap_w = k // 9, (k // 3) % 3, k % 3
    total = None
    for ref, first in ((own_ref, 2 * core), (peer_ref, 2 * (1 - core))):
        for src in range(4):
            patch = cols[tap_w, pl.ds(tap_t + first, 2), pl.ds(4 * src + tap_h, 4)]
            term = jnp.dot(ref[src], patch.reshape(256, 384), preferred_element_type=F32)
            total = term if total is None else total + term
    for q in range(4):
        out_ref[q, 0] = total[24 * q : 24 * q + 24].astype(BF)


def weight_grad(core, cols, own, peer):
    def whole(a):
        return pl.BlockSpec(a.shape, lambda j, *_: (0,) * a.ndim)

    return pl.pallas_call(
        weight_grad_kernel,
        out_shape=jax.ShapeDtypeStruct((4, N_TAPS, 24, 384), BF),
        grid_spec=pltpu.PrefetchScalarGridSpec(
            num_scalar_prefetch=1,
            grid=(N_TAPS,),
            in_specs=[whole(a) for a in (cols, own, peer)],
            out_specs=pl.BlockSpec((4, 1, 24, 384), lambda j, *_: (0, j, 0, 0)),
        ),
        compiler_params=pltpu.CompilerParams(vmem_limit_bytes=48 << 20),
        cost_estimate=pl.CostEstimate(
            flops=2 * N_TAPS * 384 * 384 * 512, bytes_accessed=9 << 20, transcendentals=0
        ),
    )(core, cols, own, peer)


def across(value, axes):
    return lax.all_to_all(value, axes, 0, 0, tiled=True)


def reduced_over_ring(mine):
    chunks = mine.astype(BF).reshape(8, 42, 384)
    got = across(chunks, RING)
    total = jnp.sum(got.astype(F32), 0).astype(BF)
    whole = across(jnp.broadcast_to(total, chunks.shape), RING)
    return whole.reshape(N_TAPS, 24, 384)


def program(frames, cache_in, kernel, conv_bias, cotangent):
    frame_count, row_count, col_count, channels = frames.shape
    core = lax.axis_index("co")
    is_first = lax.axis_index(TM) == 0
    weights = kernel.transpose(1, 2, 3, 0, 4)
    earlier = shifted(frames, TM, 1)
    earlier = jnp.where(is_first, cache_in, earlier)
    stacked = jnp.concatenate([earlier, frames], 0)
    extended = with_halo(stacked, ((HEIGHT, 1), ("z", 2)), 1)
    rows = lax.dynamic_slice(
        extended,
        (core, (lax.axis_index("y") != 0).astype(jnp.int32), 0, 0),
        (3, 5, col_count + 2, channels),
    )
    rows = jnp.pad(rows, ((0, 0), (0, 0), (0, 6), (0, 0)))
    line = [rows] + [exchanged(rows, "y", flip) for flip in (1, 3, 2)]
    pre_act = jnp.zeros((frame_count * row_count * col_count, channels), F32) + conv_bias
    for tap_t in range(3):
        for tap_h in range(3):
            for tap_w in range(3):
                block = tap_block(extended, tap_t, tap_h, tap_w, frame_count, row_count, col_count)
                pre_act = pre_act + lax.dot_general(
                    block,
                    weights[tap_t, tap_h, tap_w],
                    (((1,), (1,)), ((), ())),
                    preferred_element_type=F32,
                )
    sigma = jax.nn.sigmoid(pre_act)
    decoded = (pre_act * sigma).astype(BF).reshape(frames.shape)
    scaled = (
        cotangent.reshape(-1, channels).astype(F32) * sigma * (1.0 + pre_act * (1.0 - sigma))
    ).astype(BF)
    row = lax.broadcasted_iota(jnp.int32, (channels, channels), 0)
    col = lax.broadcasted_iota(jnp.int32, (channels, channels), 1)
    order = (row // 24 % 4 * 96 + row // 96 * 24 + row % 24 == col).astype(BF)
    own = lax.dot_general(order, scaled, (((1,), (1,)), ((), ())), preferred_element_type=F32)
    own = across(own.astype(BF).reshape(4, 96, -1), "y")
    own, *line = lax.optimization_barrier((own, *line))
    line_peer = jnp.stack([jnp.where(core == 0, v[1:3], v[0:2]) for v in line])
    line_peer = exchanged(line_peer, "co", 1)
    cols = spread(jnp.stack([core, lax.axis_index("y")]), line, line_peer)
    parts = weight_grad(core.reshape(1), cols, own, exchanged(own, "co", 1))
    scaled, parts = lax.optimization_barrier((scaled, parts))
    parts = across(parts, "x")
    mine = reduced_over_ring(jnp.sum(parts.astype(F32), 0))
    theirs = exchanged(mine, "co", 1)
    taps = jnp.where(
        core == 0,
        jnp.concatenate([mine, theirs[1:]], 0),
        jnp.concatenate([theirs, mine[1:]], 0),
    ).astype(F32)
    kernel_grad = taps.reshape(3, 3, 3, 24, channels).transpose(3, 0, 1, 2, 4)

    grad_rimmed = with_halo(scaled.reshape(frames.shape), ((HEIGHT, 1), ("z", 2)), 1)
    partial_value = jnp.zeros((frame_count + 2, row_count, col_count, channels), F32)
    for tap_t in range(3):
        contrib = jnp.zeros((frame_count * row_count * col_count, channels), F32)
        for tap_h in range(3):
            for tap_w in range(3):
                block = grad_rimmed[
                    :, 2 - tap_h : 2 - tap_h + row_count, 2 - tap_w : 2 - tap_w + col_count
                ].reshape(-1, channels)
                contrib = contrib + jnp.dot(
                    block, weights[tap_t, tap_h, tap_w], preferred_element_type=F32
                )
        partial_value = partial_value.at[tap_t : tap_t + frame_count].add(
            contrib.reshape(frame_count, row_count, col_count, channels)
        )
    cache_grad = partial_value[:2].astype(BF)
    carried = shifted(cache_grad, TM, -1)
    frame_grad = (
        partial_value[2:].at[frame_count - 2 :].add(carried.astype(F32)).astype(BF)
    )
    return (decoded, frame_grad, cache_grad, kernel_grad)


def solution(mesh):
    split = Mesh(mesh.devices.reshape(2, 2, 4, 4, 4), ("zh", "co", "x", "y", "z"))
    block = P(TM, HEIGHT, "z", None)
    return jax.shard_map(
        program,
        mesh=split,
        in_specs=(block, P(None, HEIGHT, "z", None), P(), P(), block),
        out_specs=(block, block, block, P(HEIGHT, None, None, None, None)),
        check_vma=False,
    )
```

```python
import jax
import jax.numpy as jnp
from jax import lax
from jax.experimental import pallas as pl
from jax.experimental.pallas import tpu as pltpu
from jax.sharding import Mesh, PartitionSpec as P

BF = jnp.bfloat16
F32 = jnp.float32
TM = ("zh", "co")
HEIGHT = ("x", "y")
RING = ("zh", "z")
N_TAPS = 14


def shifted(value, axis, by):
    length = lax.axis_size(axis)
    pairs = [(i, i + by) for i in range(length) if 0 <= i + by < length]
    return lax.ppermute(value, axis, pairs)


def exchanged(value, axis, flip):
    return lax.ppermute(value, axis, [(i, i ^ flip) for i in range(lax.axis_size(axis))])


def with_halo(value, sides, width):
    for axis, dim in sides:
        size, length = (lax.axis_size(axis), value.shape[dim])
        up = [(i, (i + 1) % size) for i in range(size - 1)]
        down = [(j, i) for i, j in up]
        last = lax.slice_in_dim(value, length - width, length, axis=dim)
        initial = lax.slice_in_dim(value, 0, width, axis=dim)
        before = lax.ppermute(last, axis, up)
        after = lax.ppermute(initial, axis, down)
        value = jnp.concatenate([before, value, after], axis=dim)
    return value


def tap_block(padded, tap_t, tap_h, tap_w, depth_count, row_count, col_count):
    block = padded[
        tap_t : tap_t + depth_count, tap_h : tap_h + row_count, tap_w : tap_w + col_count
    ]
    return block.reshape(-1, block.shape[-1])


def spread_kernel(where_ref, *refs):
    lines, peer_ref, out_ref = refs[:4], refs[4], refs[5]
    core = where_ref[0]
    for k, flip in enumerate((0, 1, 3, 2)):
        src = where_ref[1] ^ flip
        at = jnp.where(src == 0, 0, 1 + 4 * src)
        for c in range(3):
            for f in range(3):
                out_ref[c, f + 2 * core, pl.ds(at, 5)] = lines[k][f, :, c : c + 32, :]
            for f in range(2):
                out_ref[c, f + 3 * (1 - core), pl.ds(at, 5)] = peer_ref[k, f, :, c : c + 32, :]


def spread(where, lines, peer):
    return pl.pallas_call(
        spread_kernel,
        out_shape=jax.ShapeDtypeStruct((3, 5, 18, 32, 384), BF),
        in_specs=[pl.BlockSpec(memory_space=pltpu.SMEM)]
        + [pl.BlockSpec(memory_space=pltpu.VMEM)] * 5,
        out_specs=pl.BlockSpec(memory_space=pltpu.VMEM),
        compiler_params=pltpu.CompilerParams(vmem_limit_bytes=14 << 20),
        cost_estimate=pl.CostEstimate(flops=0, bytes_accessed=12 << 20, transcendentals=0),
    )(where, *lines, peer)


def weight_grad_kernel(core_ref, cols, own_ref, peer_ref, out_ref):
    core = core_ref[0]
    k = pl.program_id(0) + 4 * core
    tap_t, tap_h, tap_w = k // 9, (k // 3) % 3, k % 3
    total = None
    for ref, first in ((own_ref, 2 * core), (peer_ref, 2 * (1 - core))):
        for src in range(4):
            patch = cols[tap_w, pl.ds(tap_t + first, 2), pl.ds(4 * src + tap_h, 4)]
            term = jnp.dot(ref[src], patch.reshape(256, 384), preferred_element_type=F32)
            total = term if total is None else total + term
    for q in range(4):
        out_ref[q, 0] = total[24 * q : 24 * q + 24].astype(BF)


def weight_grad(core, cols, own, peer):
    return pl.pallas_call(
        weight_grad_kernel,
        out_shape=jax.ShapeDtypeStruct((4, N_TAPS, 24, 384), BF),
        grid_spec=pltpu.PrefetchScalarGridSpec(
            num_scalar_prefetch=1,
            grid=(N_TAPS,),
            in_specs=[pl.BlockSpec(memory_space=pltpu.VMEM)] * 3,
            out_specs=pl.BlockSpec((4, 1, 24, 384), lambda j, *_: (0, j, 0, 0)),
        ),
        compiler_params=pltpu.CompilerParams(vmem_limit_bytes=14 << 20),
        cost_estimate=pl.CostEstimate(
            flops=2 * N_TAPS * 384 * 384 * 512, bytes_accessed=9 << 20, transcendentals=0
        ),
    )(core, cols, own, peer)


def input_grad_kernel(rim_ref, weight_ref, head_ref, tail_ref, cols, total):
    step = pl.program_id(0)

    @pl.when(step == 0)
    def _():
        total[...] = jnp.zeros_like(total)
        for c in range(3):
            cols[c] = rim_ref[:, :, 2 - c : 34 - c, :]

    tap_t, tap_h = step // 3, step % 3
    term = None
    for c in range(3):
        block = cols[c, :, pl.ds(2 - tap_h, 4)].reshape(256, 384)
        part = jnp.dot(block, weight_ref[0, 0, c], preferred_element_type=F32)
        term = part if term is None else term + part
    total[pl.ds(tap_t, 2)] += term.reshape(2, 128, 384)

    @pl.when(step == 8)
    def _():
        head_ref[...] = total[:2].astype(BF)
        tail_ref[...] = total[2:]


def input_grad(rimmed, weights):
    def whole(shape):
        return pl.BlockSpec(shape, lambda j: (0,) * len(shape))

    return pl.pallas_call(
        input_grad_kernel,
        out_shape=[
            jax.ShapeDtypeStruct((2, 128, 384), BF),
            jax.ShapeDtypeStruct((2, 128, 384), F32),
        ],
        grid=(9,),
        in_specs=[
            pl.BlockSpec(memory_space=pltpu.VMEM),
            pl.BlockSpec((1, 1, 3, 384, 384), lambda j: (j // 3, j % 3, 0, 0, 0)),
        ],
        out_specs=[whole((2, 128, 384)), whole((2, 128, 384))],
        scratch_shapes=[pltpu.VMEM((3, 2, 6, 32, 384), BF), pltpu.VMEM((4, 128, 384), F32)],
        compiler_params=pltpu.CompilerParams(vmem_limit_bytes=60 << 20),
        cost_estimate=pl.CostEstimate(
            flops=2 * 27 * 256 * 384 * 384, bytes_accessed=9 << 20, transcendentals=0
        ),
    )(rimmed, weights)


def across(value, axes):
    return lax.all_to_all(value, axes, 0, 0, tiled=True)


def reduced_over_ring(mine):
    chunks = mine.astype(BF).reshape(8, 42, 384)
    got = across(chunks, RING)
    total = jnp.sum(got.astype(F32), 0).astype(BF)
    whole = across(jnp.broadcast_to(total, chunks.shape), RING)
    return whole.reshape(N_TAPS, 24, 384)


def program(frames, cache_in, kernel, conv_bias, cotangent):
    frame_count, row_count, col_count, channels = frames.shape
    core = lax.axis_index("co")
    is_first = lax.axis_index(TM) == 0
    row = lax.broadcasted_iota(jnp.int32, (channels, channels), 0)
    col = lax.broadcasted_iota(jnp.int32, (channels, channels), 1)
    order = (row // 24 % 4 * 96 + row // 96 * 24 + row % 24 == col).astype(BF)
    order, frames = lax.optimization_barrier((order, frames))
    weights = kernel.transpose(1, 2, 3, 0, 4)
    earlier = shifted(frames, TM, 1)
    earlier = jnp.where(is_first, cache_in, earlier)
    stacked = jnp.concatenate([earlier, frames], 0)
    extended = with_halo(stacked, ((HEIGHT, 1), ("z", 2)), 1)
    rows = lax.dynamic_slice(
        extended,
        (core, (lax.axis_index("y") != 0).astype(jnp.int32), 0, 0),
        (3, 5, col_count + 2, channels),
    )
    rows = jnp.pad(rows, ((0, 0), (0, 0), (0, 6), (0, 0)))
    near = [exchanged(rows, "y", flip) for flip in (1, 3)]
    pre_act = jnp.zeros((frame_count * row_count * col_count, channels), F32) + conv_bias
    for tap_t in range(3):
        if tap_t == 2:
            pre_act, *near = lax.optimization_barrier((pre_act, *near))
            far = [
                exchanged(near[0][:, :, :16], "y", 3),
                exchanged(near[1][:, :, 16:], "y", 1),
            ]
        for tap_h in range(3):
            for tap_w in range(3):
                block = tap_block(extended, tap_t, tap_h, tap_w, frame_count, row_count, col_count)
                pre_act = pre_act + lax.dot_general(
                    block,
                    weights[tap_t, tap_h, tap_w],
                    (((1,), (1,)), ((), ())),
                    preferred_element_type=F32,
                )
    sigma = jax.nn.sigmoid(pre_act)
    decoded = (pre_act * sigma).astype(BF).reshape(frames.shape)
    scaled = (
        cotangent.reshape(-1, channels).astype(F32) * sigma * (1.0 + pre_act * (1.0 - sigma))
    ).astype(BF)
    own = lax.dot_general(order, scaled, (((1,), (1,)), ((), ())), preferred_element_type=F32)
    own, *far = lax.optimization_barrier((own.astype(BF).reshape(4, 96, -1), *far))
    own = across(own, "y")
    line = [rows, *near, jnp.concatenate(far, 2)]
    line_peer = jnp.stack([jnp.where(core == 0, v[1:3], v[0:2]) for v in line])
    line_peer = exchanged(line_peer, "co", 1)
    cols = spread(jnp.stack([core, lax.axis_index("y")]), line, line_peer)
    parts = weight_grad(core.reshape(1), cols, own, exchanged(own, "co", 1))
    scaled, parts = lax.optimization_barrier((scaled, parts))
    parts = across(parts, "x")
    mine = reduced_over_ring(jnp.sum(parts.astype(F32), 0))
    theirs = exchanged(mine, "co", 1)
    taps = jnp.where(
        core == 0,
        jnp.concatenate([mine, theirs[1:]], 0),
        jnp.concatenate([theirs, mine[1:]], 0),
    ).astype(F32)
    kernel_grad = taps.reshape(3, 3, 3, 24, channels).transpose(3, 0, 1, 2, 4)

    tall = with_halo(scaled.reshape(frames.shape), ((HEIGHT, 1),), 1)
    left = shifted(tall[:, :, -1:], "z", 1)
    right = shifted(tall[:, :, :1], "z", -1)
    grad_rimmed = jnp.concatenate([left, tall, right], 2)
    head, tail = input_grad(grad_rimmed, weights)
    cache_grad = head.reshape(frames.shape)
    carried = shifted(cache_grad, TM, -1)
    frame_grad = (tail.reshape(frames.shape) + carried.astype(F32)).astype(BF)
    return (decoded, frame_grad, cache_grad, kernel_grad)


def solution(mesh):
    split = Mesh(mesh.devices.reshape(2, 2, 4, 4, 4), ("zh", "co", "x", "y", "z"))
    block = P(TM, HEIGHT, "z", None)
    return jax.shard_map(
        program,
        mesh=split,
        in_specs=(block, P(None, HEIGHT, "z", None), P(), P(), block),
        out_specs=(block, block, block, P(HEIGHT, None, None, None, None)),
        check_vma=False,
    )
```

```python
import jax
import jax.numpy as jnp
from jax import lax
from jax.experimental import pallas as pl
from jax.experimental.pallas import tpu as pltpu
from jax.sharding import Mesh, PartitionSpec as P

BF = jnp.bfloat16
F32 = jnp.float32
TM = ("zh", "co")
HEIGHT = ("x", "y")
RING = ("zh", "z")
N_TAPS = 14


def shifted(value, axis, by):
    length = lax.axis_size(axis)
    pairs = [(i, i + by) for i in range(length) if 0 <= i + by < length]
    return lax.ppermute(value, axis, pairs)


def exchanged(value, axis, flip):
    return lax.ppermute(value, axis, [(i, i ^ flip) for i in range(lax.axis_size(axis))])


def with_halo(value, sides, width):
    for axis, dim in sides:
        size, length = (lax.axis_size(axis), value.shape[dim])
        up = [(i, (i + 1) % size) for i in range(size - 1)]
        down = [(j, i) for i, j in up]
        last = lax.slice_in_dim(value, length - width, length, axis=dim)
        initial = lax.slice_in_dim(value, 0, width, axis=dim)
        before = lax.ppermute(last, axis, up)
        after = lax.ppermute(initial, axis, down)
        value = jnp.concatenate([before, value, after], axis=dim)
    return value


def tap_block(padded, tap_t, tap_h, tap_w, depth_count, row_count, col_count):
    block = padded[
        tap_t : tap_t + depth_count, tap_h : tap_h + row_count, tap_w : tap_w + col_count
    ]
    return block.reshape(-1, block.shape[-1])


def weight_grad_kernel(where_ref, own_ref, peer_ref, *refs):
    lines, both_ref, out_ref, cols = refs[:4], refs[4], refs[5], refs[6]
    core = where_ref[0]

    @pl.when(pl.program_id(0) == 0)
    def _():
        for n, flip in enumerate((0, 1, 3, 2)):
            src = where_ref[1] ^ flip
            at = jnp.where(src == 0, 0, 1 + 4 * src)
            for c in range(3):
                for f in range(3):
                    cols[c, f + 2 * core, pl.ds(at, 5)] = lines[n][f, :, c : c + 32, :]
                for f in range(2):
                    cols[c, f + 3 * (1 - core), pl.ds(at, 5)] = both_ref[n, f, :, c : c + 32, :]

    k = pl.program_id(0) + 4 * core
    tap_t, tap_h, tap_w = k // 9, (k // 3) % 3, k % 3
    total = None
    for ref, first in ((own_ref, 2 * core), (peer_ref, 2 * (1 - core))):
        for src in range(4):
            patch = cols[tap_w, pl.ds(tap_t + first, 2), pl.ds(4 * src + tap_h, 4)]
            term = jnp.dot(ref[src], patch.reshape(256, 384), preferred_element_type=F32)
            total = term if total is None else total + term
    for q in range(4):
        out_ref[q, 0] = total[24 * q : 24 * q + 24].astype(BF)


def weight_grad(where, own, peer, lines, both):
    return pl.pallas_call(
        weight_grad_kernel,
        out_shape=jax.ShapeDtypeStruct((4, N_TAPS, 24, 384), BF),
        grid_spec=pltpu.PrefetchScalarGridSpec(
            num_scalar_prefetch=1,
            grid=(N_TAPS,),
            in_specs=[pl.BlockSpec(memory_space=pltpu.VMEM)] * 7,
            out_specs=pl.BlockSpec((4, 1, 24, 384), lambda j, *_: (0, j, 0, 0)),
            scratch_shapes=[pltpu.VMEM((3, 5, 18, 32, 384), BF)],
        ),
        compiler_params=pltpu.CompilerParams(vmem_limit_bytes=16 << 20),
        cost_estimate=pl.CostEstimate(
            flops=2 * N_TAPS * 384 * 384 * 512, bytes_accessed=9 << 20, transcendentals=0
        ),
    )(where, own, peer, *lines, both)


def input_grad_kernel(rim_ref, weight_ref, head_ref, tail_ref, cols, total):
    step = pl.program_id(0)

    @pl.when(step == 0)
    def _():
        total[...] = jnp.zeros_like(total)
        for c in range(3):
            cols[c] = rim_ref[:, :, 2 - c : 34 - c, :]

    tap_t, tap_h = step // 3, step % 3
    term = None
    for c in range(3):
        block = cols[c, :, pl.ds(2 - tap_h, 4)].reshape(256, 384)
        part = jnp.dot(block, weight_ref[0, 0, c], preferred_element_type=F32)
        term = part if term is None else term + part
    total[pl.ds(tap_t, 2)] += term.reshape(2, 128, 384)

    @pl.when(step == 8)
    def _():
        head_ref[...] = total[:2].astype(BF)
        tail_ref[...] = total[2:]


def input_grad(rimmed, weights):
    def whole(shape):
        return pl.BlockSpec(shape, lambda j: (0,) * len(shape))

    return pl.pallas_call(
        input_grad_kernel,
        out_shape=[
            jax.ShapeDtypeStruct((2, 128, 384), BF),
            jax.ShapeDtypeStruct((2, 128, 384), F32),
        ],
        grid=(9,),
        in_specs=[
            pl.BlockSpec(memory_space=pltpu.VMEM),
            pl.BlockSpec((1, 1, 3, 384, 384), lambda j: (j // 3, j % 3, 0, 0, 0)),
        ],
        out_specs=[whole((2, 128, 384)), whole((2, 128, 384))],
        scratch_shapes=[pltpu.VMEM((3, 2, 6, 32, 384), BF), pltpu.VMEM((4, 128, 384), F32)],
        compiler_params=pltpu.CompilerParams(vmem_limit_bytes=60 << 20),
        cost_estimate=pl.CostEstimate(
            flops=2 * 27 * 256 * 384 * 384, bytes_accessed=9 << 20, transcendentals=0
        ),
    )(rimmed, weights)


def across(value, axes):
    return lax.all_to_all(value, axes, 0, 0, tiled=True)


def reduced_over_ring(mine):
    chunks = mine.astype(BF).reshape(8, 42, 384)
    got = across(chunks, RING)
    total = jnp.sum(got.astype(F32), 0).astype(BF)
    whole = across(jnp.broadcast_to(total, chunks.shape), RING)
    return whole.reshape(N_TAPS, 24, 384)


def program(frames, cache_in, kernel, conv_bias, cotangent):
    frame_count, row_count, col_count, channels = frames.shape
    core = lax.axis_index("co")
    is_first = lax.axis_index(TM) == 0
    row = lax.broadcasted_iota(jnp.int32, (channels, channels), 0)
    col = lax.broadcasted_iota(jnp.int32, (channels, channels), 1)
    order = (row // 24 % 4 * 96 + row // 96 * 24 + row % 24 == col).astype(BF)
    order, frames = lax.optimization_barrier((order, frames))
    weights = kernel.transpose(1, 2, 3, 0, 4)
    earlier = shifted(frames, TM, 1)
    earlier = jnp.where(is_first, cache_in, earlier)
    stacked = jnp.concatenate([earlier, frames], 0)
    extended = with_halo(stacked, ((HEIGHT, 1), ("z", 2)), 1)
    rows = lax.dynamic_slice(
        extended,
        (core, (lax.axis_index("y") != 0).astype(jnp.int32), 0, 0),
        (3, 5, col_count + 2, channels),
    )
    rows = jnp.pad(rows, ((0, 0), (0, 0), (0, 6), (0, 0)))
    near = [exchanged(rows, "y", flip) for flip in (1, 3)]
    pre_act = jnp.zeros((frame_count * row_count * col_count, channels), F32) + conv_bias
    for tap_t in range(3):
        if tap_t == 2:
            pre_act, *near = lax.optimization_barrier((pre_act, *near))
            far = [
                exchanged(near[0][:, :, :16], "y", 3),
                exchanged(near[1][:, :, 16:], "y", 1),
            ]
        for tap_h in range(3):
            for tap_w in range(3):
                block = tap_block(extended, tap_t, tap_h, tap_w, frame_count, row_count, col_count)
                pre_act = pre_act + lax.dot_general(
                    block,
                    weights[tap_t, tap_h, tap_w],
                    (((1,), (1,)), ((), ())),
                    preferred_element_type=F32,
                )
    sigma = jax.nn.sigmoid(pre_act)
    decoded = (pre_act * sigma).astype(BF).reshape(frames.shape)
    scaled = (
        cotangent.reshape(-1, channels).astype(F32) * sigma * (1.0 + pre_act * (1.0 - sigma))
    ).astype(BF)
    own = lax.dot_general(order, scaled, (((1,), (1,)), ((), ())), preferred_element_type=F32)
    own, *far = lax.optimization_barrier((own.astype(BF).reshape(4, 96, -1), *far))
    own = across(own, "y")
    line = [rows, *near, jnp.concatenate(far, 2)]
    line_peer = jnp.stack([jnp.where(core == 0, v[1:3], v[0:2]) for v in line])
    line_peer = exchanged(line_peer, "co", 1)
    scaled_rows = scaled.reshape(frames.shape)
    above = shifted(scaled_rows[:, -1:], HEIGHT, 1)
    below = shifted(scaled_rows[:, :1], HEIGHT, -1)
    line_peer, above, below = lax.optimization_barrier((line_peer, above, below))
    where = jnp.stack([core, lax.axis_index("y")])
    parts = weight_grad(where, own, exchanged(own, "co", 1), line, line_peer)
    parts = across(parts, "x")
    mine = reduced_over_ring(jnp.sum(parts.astype(F32), 0))
    theirs = exchanged(mine, "co", 1)
    taps = jnp.where(
        core == 0,
        jnp.concatenate([mine, theirs[1:]], 0),
        jnp.concatenate([theirs, mine[1:]], 0),
    ).astype(F32)
    kernel_grad = taps.reshape(3, 3, 3, 24, channels).transpose(3, 0, 1, 2, 4)

    tall = jnp.concatenate([above, scaled_rows, below], 1)
    left = shifted(tall[:, :, -1:], "z", 1)
    right = shifted(tall[:, :, :1], "z", -1)
    grad_rimmed = jnp.concatenate([left, tall, right], 2)
    head, tail = input_grad(grad_rimmed, weights)
    cache_grad = head.reshape(frames.shape)
    carried = shifted(cache_grad, TM, -1)
    frame_grad = (tail.reshape(frames.shape) + carried.astype(F32)).astype(BF)
    return (decoded, frame_grad, cache_grad, kernel_grad)


def solution(mesh):
    split = Mesh(mesh.devices.reshape(2, 2, 4, 4, 4), ("zh", "co", "x", "y", "z"))
    block = P(TM, HEIGHT, "z", None)
    return jax.shard_map(
        program,
        mesh=split,
        in_specs=(block, P(None, HEIGHT, "z", None), P(), P(), block),
        out_specs=(block, block, block, P(HEIGHT, None, None, None, None)),
        check_vma=False,
    )
```

```python
import jax
import jax.numpy as jnp
from jax import lax
from jax.experimental import pallas as pl
from jax.experimental.pallas import tpu as pltpu
from jax.sharding import Mesh, PartitionSpec as P

BF = jnp.bfloat16
F32 = jnp.float32
TM = ("zh", "co")
HEIGHT = ("x", "y")
RING = ("zh", "z")
N_TAPS = 14


def shifted(value, axis, by):
    length = lax.axis_size(axis)
    pairs = [(i, i + by) for i in range(length) if 0 <= i + by < length]
    return lax.ppermute(value, axis, pairs)


def exchanged(value, axis, flip):
    return lax.ppermute(value, axis, [(i, i ^ flip) for i in range(lax.axis_size(axis))])


def with_halo(value, sides, width):
    for axis, dim in sides:
        size, length = (lax.axis_size(axis), value.shape[dim])
        up = [(i, (i + 1) % size) for i in range(size - 1)]
        down = [(j, i) for i, j in up]
        last = lax.slice_in_dim(value, length - width, length, axis=dim)
        initial = lax.slice_in_dim(value, 0, width, axis=dim)
        before = lax.ppermute(last, axis, up)
        after = lax.ppermute(initial, axis, down)
        value = jnp.concatenate([before, value, after], axis=dim)
    return value


def whole(shape):
    return pl.BlockSpec(shape, lambda j: (0,) * len(shape))


def three_taps(cols, frame, tap_h, weight_ref):
    total = None
    for c in range(3):
        block = cols[c, pl.ds(frame, 2), pl.ds(tap_h, 4)].reshape(256, 384)
        term = lax.dot_general(
            block, weight_ref[0, 0, c], (((1,), (1,)), ((), ())), preferred_element_type=F32
        )
        total = term if total is None else total + term
    return total


def forward_own_kernel(own_ref, bias_ref, weight_ref, out_ref, cols):
    tap_h = pl.program_id(0)

    @pl.when(tap_h == 0)
    def _():
        out_ref[...] = jnp.broadcast_to(bias_ref[...], out_ref.shape)
        for c in range(3):
            cols[c] = own_ref[:, :, c : c + 32, :]

    out_ref[...] += three_taps(cols, 0, tap_h, weight_ref)


def forward_own(own_ext, bias, weights):
    return pl.pallas_call(
        forward_own_kernel,
        out_shape=jax.ShapeDtypeStruct((256, 384), F32),
        grid=(3,),
        in_specs=[
            pl.BlockSpec(memory_space=pltpu.VMEM),
            whole((1, 384)),
            pl.BlockSpec((1, 1, 3, 384, 384), lambda j: (2, j, 0, 0, 0)),
        ],
        out_specs=whole((256, 384)),
        scratch_shapes=[pltpu.VMEM((3, 2, 6, 32, 384), BF)],
        compiler_params=pltpu.CompilerParams(vmem_limit_bytes=60 << 20),
        cost_estimate=pl.CostEstimate(
            flops=2 * 9 * 256 * 384 * 384, bytes_accessed=3 << 20, transcendentals=0
        ),
    )(own_ext, bias.reshape(1, -1), weights)


def forward_rest_kernel(
    early_ref, own_ref, so_far_ref, cotangent_ref, order_ref, weight_ref,
    decoded_ref, scaled_ref, turned_ref, cols, total,
):
    step = pl.program_id(0)

    @pl.when(step == 0)
    def _():
        total[...] = so_far_ref[...]
        for c in range(3):
            cols[c, :2] = early_ref[:, :, c : c + 32, :]
            cols[c, 2] = own_ref[0, :, c : c + 32, :]

    total[...] += three_taps(cols, 1 - step // 3, step % 3, weight_ref)

    @pl.when(step == 5)
    def _():
        pre_act = total[...]
        sigma = jax.nn.sigmoid(pre_act)
        decoded_ref[...] = (pre_act * sigma).astype(BF)
        scaled = cotangent_ref[...].astype(F32) * sigma * (1.0 + pre_act * (1.0 - sigma))
        scaled_ref[...] = scaled.astype(BF)
        turned_ref[...] = lax.dot_general(
            order_ref[...], scaled.astype(BF), (((1,), (1,)), ((), ())), preferred_element_type=F32
        ).astype(BF)


def forward_rest(early_ext, own_ext, so_far, cotangent, order, weights):
    return pl.pallas_call(
        forward_rest_kernel,
        out_shape=[
            jax.ShapeDtypeStruct((256, 384), BF),
            jax.ShapeDtypeStruct((256, 384), BF),
            jax.ShapeDtypeStruct((384, 256), BF),
        ],
        grid=(6,),
        in_specs=[pl.BlockSpec(memory_space=pltpu.VMEM)] * 5
        + [pl.BlockSpec((1, 1, 3, 384, 384), lambda j: (1 - j // 3, j % 3, 0, 0, 0))],
        out_specs=[whole((256, 384)), whole((256, 384)), whole((384, 256))],
        scratch_shapes=[pltpu.VMEM((3, 3, 6, 32, 384), BF), pltpu.VMEM((256, 384), F32)],
        compiler_params=pltpu.CompilerParams(vmem_limit_bytes=60 << 20),
        cost_estimate=pl.CostEstimate(
            flops=2 * 18 * 256 * 384 * 384, bytes_accessed=6 << 20, transcendentals=1 << 17
        ),
    )(early_ext, own_ext, so_far, cotangent, order, weights)


def weight_grad_kernel(where_ref, own_ref, peer_ref, *refs):
    lines, both_ref, out_ref, cols = refs[:4], refs[4], refs[5], refs[6]
    core = where_ref[0]

    @pl.when(pl.program_id(0) == 0)
    def _():
        for n, flip in enumerate((0, 1, 3, 2)):
            src = where_ref[1] ^ flip
            at = jnp.where(src == 0, 0, 1 + 4 * src)
            for c in range(3):
                for f in range(3):
                    cols[c, f + 2 * core, pl.ds(at, 5)] = lines[n][f, :, c : c + 32, :]
                for f in range(2):
                    cols[c, f + 3 * (1 - core), pl.ds(at, 5)] = both_ref[n, f, :, c : c + 32, :]

    k = pl.program_id(0) + 4 * core
    tap_t, tap_h, tap_w = k // 9, (k // 3) % 3, k % 3
    total = None
    for ref, first in ((own_ref, 2 * core), (peer_ref, 2 * (1 - core))):
        for src in range(4):
            patch = cols[tap_w, pl.ds(tap_t + first, 2), pl.ds(4 * src + tap_h, 4)]
            term = jnp.dot(ref[src], patch.reshape(256, 384), preferred_element_type=F32)
            total = term if total is None else total + term
    for q in range(4):
        out_ref[q, 0] = total[24 * q : 24 * q + 24].astype(BF)


def weight_grad(where, own, peer, lines, both):
    return pl.pallas_call(
        weight_grad_kernel,
        out_shape=jax.ShapeDtypeStruct((4, N_TAPS, 24, 384), BF),
        grid_spec=pltpu.PrefetchScalarGridSpec(
            num_scalar_prefetch=1,
            grid=(N_TAPS,),
            in_specs=[pl.BlockSpec(memory_space=pltpu.VMEM)] * 7,
            out_specs=pl.BlockSpec((4, 1, 24, 384), lambda j, *_: (0, j, 0, 0)),
            scratch_shapes=[pltpu.VMEM((3, 5, 18, 32, 384), BF)],
        ),
        compiler_params=pltpu.CompilerParams(vmem_limit_bytes=16 << 20),
        cost_estimate=pl.CostEstimate(
            flops=2 * N_TAPS * 384 * 384 * 512, bytes_accessed=9 << 20, transcendentals=0
        ),
    )(where, own, peer, *lines, both)


def input_grad_kernel(rim_ref, weight_ref, head_ref, tail_ref, cols, total):
    step = pl.program_id(0)

    @pl.when(step == 0)
    def _():
        total[...] = jnp.zeros_like(total)
        for c in range(3):
            cols[c] = rim_ref[:, :, 2 - c : 34 - c, :]

    tap_t, tap_h = step // 3, step % 3
    term = None
    for c in range(3):
        block = cols[c, :, pl.ds(2 - tap_h, 4)].reshape(256, 384)
        part = jnp.dot(block, weight_ref[0, 0, c], preferred_element_type=F32)
        term = part if term is None else term + part
    total[pl.ds(tap_t, 2)] += term.reshape(2, 128, 384)

    @pl.when(step == 8)
    def _():
        head_ref[...] = total[:2].astype(BF)
        tail_ref[...] = total[2:]


def input_grad(rimmed, weights):
    return pl.pallas_call(
        input_grad_kernel,
        out_shape=[
            jax.ShapeDtypeStruct((2, 128, 384), BF),
            jax.ShapeDtypeStruct((2, 128, 384), F32),
        ],
        grid=(9,),
        in_specs=[
            pl.BlockSpec(memory_space=pltpu.VMEM),
            pl.BlockSpec((1, 1, 3, 384, 384), lambda j: (j // 3, j % 3, 0, 0, 0)),
        ],
        out_specs=[whole((2, 128, 384)), whole((2, 128, 384))],
        scratch_shapes=[pltpu.VMEM((3, 2, 6, 32, 384), BF), pltpu.VMEM((4, 128, 384), F32)],
        compiler_params=pltpu.CompilerParams(vmem_limit_bytes=60 << 20),
        cost_estimate=pl.CostEstimate(
            flops=2 * 27 * 256 * 384 * 384, bytes_accessed=9 << 20, transcendentals=0
        ),
    )(rimmed, weights)


def across(value, axes):
    return lax.all_to_all(value, axes, 0, 0, tiled=True)


def reduced_over_ring(mine):
    chunks = mine.astype(BF).reshape(8, 42, 384)
    got = across(chunks, RING)
    total = jnp.sum(got.astype(F32), 0).astype(BF)
    whole = across(jnp.broadcast_to(total, chunks.shape), RING)
    return whole.reshape(N_TAPS, 24, 384)


def program(frames, cache_in, kernel, conv_bias, cotangent):
    _, _, col_count, channels = frames.shape
    core = lax.axis_index("co")
    is_first = lax.axis_index(TM) == 0
    row = lax.broadcasted_iota(jnp.int32, (channels, channels), 0)
    col = lax.broadcasted_iota(jnp.int32, (channels, channels), 1)
    order = (row // 24 % 4 * 96 + row // 96 * 24 + row % 24 == col).astype(BF)
    order, frames = lax.optimization_barrier((order, frames))
    weights = kernel.transpose(1, 2, 3, 0, 4)
    own_ext = with_halo(frames, ((HEIGHT, 1),), 1)
    earlier = shifted(frames, TM, 1)
    own_ext = with_halo(own_ext, (("z", 2),), 1)
    so_far = forward_own(own_ext, conv_bias, weights)
    earlier = jnp.where(is_first, cache_in, earlier)
    early_ext = with_halo(earlier, ((HEIGHT, 1), ("z", 2)), 1)
    extended = jnp.concatenate([early_ext, own_ext], 0)
    rows = lax.dynamic_slice(
        extended,
        (core, (lax.axis_index("y") != 0).astype(jnp.int32), 0, 0),
        (3, 5, col_count + 2, channels),
    )
    rows = jnp.pad(rows, ((0, 0), (0, 0), (0, 6), (0, 0)))
    near = [exchanged(rows, "y", flip) for flip in (1, 3)]
    decoded, scaled, own = forward_rest(
        early_ext, own_ext, so_far, cotangent.reshape(-1, channels), order, weights
    )
    decoded = decoded.reshape(frames.shape)
    own = own.reshape(4, 96, -1)
    own = across(own, "y")
    far = [exchanged(near[0][:, :, :16], "y", 3), exchanged(near[1][:, :, 16:], "y", 1)]
    line = [rows, *near, jnp.concatenate(far, 2)]
    line_peer = jnp.stack([jnp.where(core == 0, v[1:3], v[0:2]) for v in line])
    line_peer = exchanged(line_peer, "co", 1)
    scaled_rows = scaled.reshape(frames.shape)
    above = shifted(scaled_rows[:, -1:], HEIGHT, 1)
    below = shifted(scaled_rows[:, :1], HEIGHT, -1)
    where = jnp.stack([core, lax.axis_index("y")])
    own_peer = exchanged(own, "co", 1)
    parts = weight_grad(where, own, own_peer, line, line_peer)
    parts = across(parts, "x")
    mine = reduced_over_ring(jnp.sum(parts.astype(F32), 0))
    theirs = exchanged(mine, "co", 1)
    taps = jnp.where(
        core == 0,
        jnp.concatenate([mine, theirs[1:]], 0),
        jnp.concatenate([theirs, mine[1:]], 0),
    ).astype(F32)
    kernel_grad = taps.reshape(3, 3, 3, 24, channels).transpose(3, 0, 1, 2, 4)

    tall = jnp.concatenate([above, scaled_rows, below], 1)
    left = shifted(tall[:, :, -1:], "z", 1)
    right = shifted(tall[:, :, :1], "z", -1)
    grad_rimmed = jnp.concatenate([left, tall, right], 2)
    head, tail = input_grad(grad_rimmed, weights)
    cache_grad = head.reshape(frames.shape)
    carried = shifted(cache_grad, TM, -1)
    frame_grad = (tail.reshape(frames.shape) + carried.astype(F32)).astype(BF)
    return (decoded, frame_grad, cache_grad, kernel_grad)


def solution(mesh):
    split = Mesh(mesh.devices.reshape(2, 2, 4, 4, 4), ("zh", "co", "x", "y", "z"))
    block = P(TM, HEIGHT, "z", None)
    return jax.shard_map(
        program,
        mesh=split,
        in_specs=(block, P(None, HEIGHT, "z", None), P(), P(), block),
        out_specs=(block, block, block, P(HEIGHT, None, None, None, None)),
        check_vma=False,
    )
```

```python
import jax
import jax.numpy as jnp
from jax import lax
from jax.experimental import pallas as pl
from jax.experimental.pallas import tpu as pltpu
from jax.sharding import Mesh, PartitionSpec as P

BF = jnp.bfloat16
F32 = jnp.float32
TM = ("zh", "co")
HEIGHT = ("x", "y")
RING = ("zh", "z")
N_TAPS = 14


def shifted(value, axis, by):
    length = lax.axis_size(axis)
    pairs = [(i, i + by) for i in range(length) if 0 <= i + by < length]
    return lax.ppermute(value, axis, pairs)


def exchanged(value, axis, flip):
    return lax.ppermute(value, axis, [(i, i ^ flip) for i in range(lax.axis_size(axis))])


def with_halo(value, sides, width):
    for axis, dim in sides:
        size, length = (lax.axis_size(axis), value.shape[dim])
        up = [(i, (i + 1) % size) for i in range(size - 1)]
        down = [(j, i) for i, j in up]
        last = lax.slice_in_dim(value, length - width, length, axis=dim)
        initial = lax.slice_in_dim(value, 0, width, axis=dim)
        before = lax.ppermute(last, axis, up)
        after = lax.ppermute(initial, axis, down)
        value = jnp.concatenate([before, value, after], axis=dim)
    return value


def tap_block(padded, tap_t, tap_h, tap_w, depth_count, row_count, col_count):
    block = padded[
        tap_t : tap_t + depth_count, tap_h : tap_h + row_count, tap_w : tap_w + col_count
    ]
    return block.reshape(-1, block.shape[-1])


def weight_grad_kernel(where_ref, scaled_ref, *refs):
    lines, both_ref, out_ref, cols = refs[:4], refs[4], refs[5], refs[6]
    core = where_ref[0]

    @pl.when(pl.program_id(0) == 0)
    def _():
        for n, flip in enumerate((0, 1, 3, 2)):
            src = where_ref[1] ^ flip
            at = jnp.where(src == 0, 0, 1 + 4 * src)
            for c in range(3):
                for f in range(3):
                    cols[c, f + 2 * core, pl.ds(at, 5)] = lines[n][f, :, c : c + 32, :]
                for f in range(2):
                    cols[c, f + 3 * (1 - core), pl.ds(at, 5)] = both_ref[n, f, :, c : c + 32, :]

    k = pl.program_id(0) + 4 * core
    tap_t, tap_h, tap_w = k // 9, (k // 3) % 3, k % 3
    total = None
    for src in range(8):
        patch = cols[tap_w, pl.ds(tap_t + src // 4 * 2, 2), pl.ds(src % 4 * 4 + tap_h, 4)]
        term = jnp.dot(scaled_ref[src], patch.reshape(256, 384), preferred_element_type=F32)
        total = term if total is None else total + term
    for q in range(4):
        out_ref[q, 0] = total[24 * q : 24 * q + 24].astype(BF)


def weight_grad(where, scaled, lines, both):
    return pl.pallas_call(
        weight_grad_kernel,
        out_shape=jax.ShapeDtypeStruct((4, N_TAPS, 24, 384), BF),
        grid_spec=pltpu.PrefetchScalarGridSpec(
            num_scalar_prefetch=1,
            grid=(N_TAPS,),
            in_specs=[pl.BlockSpec(memory_space=pltpu.VMEM)] * 6,
            out_specs=pl.BlockSpec((4, 1, 24, 384), lambda j, *_: (0, j, 0, 0)),
            scratch_shapes=[pltpu.VMEM((3, 5, 18, 32, 384), BF)],
        ),
        compiler_params=pltpu.CompilerParams(vmem_limit_bytes=16 << 20),
        cost_estimate=pl.CostEstimate(
            flops=2 * N_TAPS * 384 * 384 * 512, bytes_accessed=9 << 20, transcendentals=0
        ),
    )(where, scaled, *lines, both)


def input_grad_kernel(rim_ref, weight_ref, head_ref, tail_ref, cols, total):
    step = pl.program_id(0)

    @pl.when(step == 0)
    def _():
        total[...] = jnp.zeros_like(total)
        for c in range(3):
            cols[c] = rim_ref[:, :, 2 - c : 34 - c, :]

    tap_t, tap_h = step // 3, step % 3
    term = None
    for c in range(3):
        block = cols[c, :, pl.ds(2 - tap_h, 4)].reshape(256, 384)
        part = jnp.dot(block, weight_ref[0, 0, c], preferred_element_type=F32)
        term = part if term is None else term + part
    total[pl.ds(tap_t, 2)] += term.reshape(2, 128, 384)

    @pl.when(step == 8)
    def _():
        head_ref[...] = total[:2].astype(BF)
        tail_ref[...] = total[2:]


def input_grad(rimmed, weights):
    def whole(shape):
        return pl.BlockSpec(shape, lambda j: (0,) * len(shape))

    return pl.pallas_call(
        input_grad_kernel,
        out_shape=[
            jax.ShapeDtypeStruct((2, 128, 384), BF),
            jax.ShapeDtypeStruct((2, 128, 384), F32),
        ],
        grid=(9,),
        in_specs=[
            pl.BlockSpec(memory_space=pltpu.VMEM),
            pl.BlockSpec((1, 1, 3, 384, 384), lambda j: (j // 3, j % 3, 0, 0, 0)),
        ],
        out_specs=[whole((2, 128, 384)), whole((2, 128, 384))],
        scratch_shapes=[pltpu.VMEM((3, 2, 6, 32, 384), BF), pltpu.VMEM((4, 128, 384), F32)],
        compiler_params=pltpu.CompilerParams(vmem_limit_bytes=60 << 20),
        cost_estimate=pl.CostEstimate(
            flops=2 * 27 * 256 * 384 * 384, bytes_accessed=9 << 20, transcendentals=0
        ),
    )(rimmed, weights)


def across(value, axes):
    return lax.all_to_all(value, axes, 0, 0, tiled=True)


def reduced_over_ring(mine):
    chunks = mine.astype(BF).reshape(8, 42, 384)
    got = across(chunks, RING)
    total = jnp.sum(got.astype(F32), 0).astype(BF)
    whole = across(jnp.broadcast_to(total, chunks.shape), RING)
    return whole.reshape(N_TAPS, 24, 384)


def program(frames, cache_in, kernel, conv_bias, cotangent):
    frame_count, row_count, col_count, channels = frames.shape
    core = lax.axis_index("co")
    is_first = lax.axis_index(TM) == 0
    row = lax.broadcasted_iota(jnp.int32, (channels, channels), 0)
    col = lax.broadcasted_iota(jnp.int32, (channels, channels), 1)
    order = (row // 24 % 4 * 96 + row // 96 * 24 + row % 24 == col).astype(BF)
    order, frames = lax.optimization_barrier((order, frames))
    weights = kernel.transpose(1, 2, 3, 0, 4)
    earlier = shifted(frames, TM, 1)
    earlier = jnp.where(is_first, cache_in, earlier)
    stacked = jnp.concatenate([earlier, frames], 0)
    extended = with_halo(stacked, ((HEIGHT, 1), ("z", 2)), 1)
    rows = lax.dynamic_slice(
        extended,
        (core, (lax.axis_index("y") != 0).astype(jnp.int32), 0, 0),
        (3, 5, col_count + 2, channels),
    )
    rows = jnp.pad(rows, ((0, 0), (0, 0), (0, 6), (0, 0)))
    near = [exchanged(rows, "y", flip) for flip in (1, 3)]
    pre_act = jnp.zeros((frame_count * row_count * col_count, channels), F32) + conv_bias
    for tap_t in range(3):
        if tap_t == 2:
            pre_act, *near = lax.optimization_barrier((pre_act, *near))
            far = [
                exchanged(near[0][:, :, :16], "y", 3),
                exchanged(near[1][:, :, 16:], "y", 1),
            ]
        for tap_h in range(3):
            for tap_w in range(3):
                block = tap_block(extended, tap_t, tap_h, tap_w, frame_count, row_count, col_count)
                pre_act = pre_act + lax.dot_general(
                    block,
                    weights[tap_t, tap_h, tap_w],
                    (((1,), (1,)), ((), ())),
                    preferred_element_type=F32,
                )
    sigma = jax.nn.sigmoid(pre_act)
    decoded = (pre_act * sigma).astype(BF).reshape(frames.shape)
    scaled = (
        cotangent.reshape(-1, channels).astype(F32) * sigma * (1.0 + pre_act * (1.0 - sigma))
    ).astype(BF)
    own = lax.dot_general(order, scaled, (((1,), (1,)), ((), ())), preferred_element_type=F32)
    own, *far = lax.optimization_barrier((own.astype(BF).reshape(4, 96, -1), *far))
    both = across(jnp.concatenate([own, own]), ("co", "y"))
    line = [rows, *near, jnp.concatenate(far, 2)]
    line_peer = jnp.stack([jnp.where(core == 0, v[1:3], v[0:2]) for v in line])
    line_peer = exchanged(line_peer, "co", 1)
    scaled_rows = scaled.reshape(frames.shape)
    above = shifted(scaled_rows[:, -1:], HEIGHT, 1)
    below = shifted(scaled_rows[:, :1], HEIGHT, -1)
    where = jnp.stack([core, lax.axis_index("y")])
    parts = weight_grad(where, both, line, line_peer)
    parts = across(parts, "x")
    mine = reduced_over_ring(jnp.sum(parts.astype(F32), 0))
    theirs = exchanged(mine, "co", 1)
    taps = jnp.where(
        core == 0,
        jnp.concatenate([mine, theirs[1:]], 0),
        jnp.concatenate([theirs, mine[1:]], 0),
    ).astype(F32)
    kernel_grad = taps.reshape(3, 3, 3, 24, channels).transpose(3, 0, 1, 2, 4)

    tall = jnp.concatenate([above, scaled_rows, below], 1)
    left = shifted(tall[:, :, -1:], "z", 1)
    right = shifted(tall[:, :, :1], "z", -1)
    grad_rimmed = jnp.concatenate([left, tall, right], 2)
    head, tail = input_grad(grad_rimmed, weights)
    cache_grad = head.reshape(frames.shape)
    carried = shifted(cache_grad, TM, -1)
    frame_grad = (tail.reshape(frames.shape) + carried.astype(F32)).astype(BF)
    return (decoded, frame_grad, cache_grad, kernel_grad)


def solution(mesh):
    split = Mesh(mesh.devices.reshape(2, 2, 4, 4, 4), ("zh", "co", "x", "y", "z"))
    block = P(TM, HEIGHT, "z", None)
    return jax.shard_map(
        program,
        mesh=split,
        in_specs=(block, P(None, HEIGHT, "z", None), P(), P(), block),
        out_specs=(block, block, block, P(HEIGHT, None, None, None, None)),
        check_vma=False,
    )
```

```python
import functools

import jax
import jax.numpy as jnp
from jax import lax
from jax.experimental import pallas as pl
from jax.experimental.pallas import tpu as pltpu
from jax.sharding import Mesh, PartitionSpec as P

BF = jnp.bfloat16
F32 = jnp.float32
TM = ("zh", "co")
HEIGHT = ("x", "y")
RING = ("zh", "z")
N_TAPS = 14


def shifted(value, axis, by):
    length = lax.axis_size(axis)
    pairs = [(i, i + by) for i in range(length) if 0 <= i + by < length]
    return lax.ppermute(value, axis, pairs)


def exchanged(value, axis, flip):
    return lax.ppermute(value, axis, [(i, i ^ flip) for i in range(lax.axis_size(axis))])


def with_halo(value, sides, width):
    for axis, dim in sides:
        size, length = (lax.axis_size(axis), value.shape[dim])
        up = [(i, (i + 1) % size) for i in range(size - 1)]
        down = [(j, i) for i, j in up]
        last = lax.slice_in_dim(value, length - width, length, axis=dim)
        initial = lax.slice_in_dim(value, 0, width, axis=dim)
        before = lax.ppermute(last, axis, up)
        after = lax.ppermute(initial, axis, down)
        value = jnp.concatenate([before, value, after], axis=dim)
    return value


def tap_block(padded, tap_t, tap_h, tap_w, depth_count, row_count, col_count):
    block = padded[
        tap_t : tap_t + depth_count, tap_h : tap_h + row_count, tap_w : tap_w + col_count
    ]
    return block.reshape(-1, block.shape[-1])


def weight_grad_kernel(where_ref, scaled_ref, *refs):
    lines, both_ref, out_ref, cols = refs[:4], refs[4], refs[5], refs[6]
    core = where_ref[0]

    @pl.when(pl.program_id(0) == 0)
    def _():
        for n, flip in enumerate((0, 1, 3, 2)):
            src = where_ref[1] ^ flip
            at = jnp.where(src == 0, 0, 1 + 4 * src)
            for c in range(3):
                for f in range(3):
                    cols[c, f + 2 * core, pl.ds(at, 5)] = lines[n][f, :, c : c + 32, :]
                for f in range(2):
                    cols[c, f + 3 * (1 - core), pl.ds(at, 5)] = both_ref[n, f, :, c : c + 32, :]

    total = None
    taps = [2 * pl.program_id(0) + n + 4 * core for n in range(2)]
    for src in range(8):
        patch = jnp.concatenate(
            [
                cols[k % 3, pl.ds(k // 9 + src // 4 * 2, 2), pl.ds(src % 4 * 4 + k // 3 % 3, 4)]
                .reshape(256, 384)
                for k in taps
            ],
            1,
        )
        term = jnp.dot(scaled_ref[src], patch, preferred_element_type=F32)
        total = term if total is None else total + term
    for n in range(2):
        for q in range(4):
            out_ref[q, n] = total[24 * q : 24 * q + 24, 384 * n : 384 * n + 384].astype(BF)


def weight_grad(where, scaled, lines, both):
    return pl.pallas_call(
        weight_grad_kernel,
        out_shape=jax.ShapeDtypeStruct((4, N_TAPS, 24, 384), BF),
        grid_spec=pltpu.PrefetchScalarGridSpec(
            num_scalar_prefetch=1,
            grid=(N_TAPS // 2,),
            in_specs=[pl.BlockSpec(memory_space=pltpu.VMEM)] * 6,
            out_specs=pl.BlockSpec((4, 2, 24, 384), lambda j, *_: (0, j, 0, 0)),
            scratch_shapes=[pltpu.VMEM((3, 5, 18, 32, 384), BF)],
        ),
        compiler_params=pltpu.CompilerParams(vmem_limit_bytes=16 << 20),
        cost_estimate=pl.CostEstimate(
            flops=2 * N_TAPS * 384 * 384 * 512, bytes_accessed=9 << 20, transcendentals=0
        ),
    )(where, scaled, *lines, both)


def input_grad_kernel(one_frame, one_slot, rim_ref, *refs):
    more, weight_ref, out_ref, cols, total = refs[:-4], refs[-4], refs[-3], refs[-2], refs[-1]
    step = pl.program_id(0)

    @pl.when(step == 0)
    def _():
        total[...] = jnp.zeros_like(total)
        for c in range(3):
            cols[c] = rim_ref[:, :, 2 - c : 34 - c, :]

    rows = pl.ds(2 - step % 3, 4)
    weight = weight_ref[0, 0].reshape(1152, 384)

    @pl.when(step < 3)
    def _():
        block = jnp.concatenate([cols[c, :, rows].reshape(256, 384) for c in range(3)], 1)
        term = jnp.dot(block, weight, preferred_element_type=F32)
        total[...] += term.reshape(2, 128, 384)

    @pl.when(step >= 3)
    def _():
        block = jnp.concatenate([cols[c, one_frame, rows].reshape(128, 384) for c in range(3)], 1)
        total[one_slot] += jnp.dot(block, weight, preferred_element_type=F32)

    @pl.when(step == 5)
    def _():
        result = total[...]
        for ref in more:
            result = result + ref[...].astype(F32)
        out_ref[...] = result.astype(BF)


def input_grad(rimmed, weights, tap_t, one_frame, one_slot, more=()):
    return pl.pallas_call(
        functools.partial(input_grad_kernel, one_frame, one_slot),
        out_shape=jax.ShapeDtypeStruct((2, 128, 384), BF),
        grid=(6,),
        in_specs=[pl.BlockSpec(memory_space=pltpu.VMEM)] * (1 + len(more))
        + [
            pl.BlockSpec(
                (1, 1, 3, 384, 384), lambda j: (jnp.where(j < 3, tap_t, 1), j % 3, 0, 0, 0)
            )
        ],
        out_specs=pl.BlockSpec((2, 128, 384), lambda j: (0, 0, 0)),
        scratch_shapes=[pltpu.VMEM((3, 2, 6, 32, 384), BF), pltpu.VMEM((2, 128, 384), F32)],
        compiler_params=pltpu.CompilerParams(vmem_limit_bytes=60 << 20),
        cost_estimate=pl.CostEstimate(
            flops=27 * 256 * 384 * 384, bytes_accessed=6 << 20, transcendentals=0
        ),
    )(rimmed, *more, weights)


def across(value, axes):
    return lax.all_to_all(value, axes, 0, 0, tiled=True)


def reduced_over_ring(mine):
    chunks = mine.astype(BF).reshape(8, 42, 384)
    got = across(chunks, RING)
    total = jnp.sum(got.astype(F32), 0).astype(BF)
    whole = across(jnp.broadcast_to(total, chunks.shape), RING)
    return whole.reshape(N_TAPS, 24, 384)


def program(frames, cache_in, kernel, conv_bias, cotangent):
    frame_count, row_count, col_count, channels = frames.shape
    core = lax.axis_index("co")
    is_first = lax.axis_index(TM) == 0
    row = lax.broadcasted_iota(jnp.int32, (channels, channels), 0)
    col = lax.broadcasted_iota(jnp.int32, (channels, channels), 1)
    order = (row // 24 % 4 * 96 + row // 96 * 24 + row % 24 == col).astype(BF)
    order, frames = lax.optimization_barrier((order, frames))
    weights = kernel.transpose(1, 2, 3, 0, 4)
    earlier = shifted(frames, TM, 1)
    earlier = jnp.where(is_first, cache_in, earlier)
    stacked = jnp.concatenate([earlier, frames], 0)
    extended = with_halo(stacked, ((HEIGHT, 1), ("z", 2)), 1)
    rows = lax.dynamic_slice(
        extended,
        (core, (lax.axis_index("y") != 0).astype(jnp.int32), 0, 0),
        (3, 5, col_count + 2, channels),
    )
    rows = jnp.pad(rows, ((0, 0), (0, 0), (0, 6), (0, 0)))
    near = [exchanged(rows, "y", flip) for flip in (1, 3)]
    pre_act = jnp.zeros((frame_count * row_count * col_count, channels), F32) + conv_bias
    for tap_t in range(3):
        if tap_t == 2:
            pre_act, *near = lax.optimization_barrier((pre_act, *near))
            far = [
                exchanged(near[0][:, :, :16], "y", 3),
                exchanged(near[1][:, :, 16:], "y", 1),
            ]
        for tap_h in range(3):
            for tap_w in range(3):
                block = tap_block(extended, tap_t, tap_h, tap_w, frame_count, row_count, col_count)
                pre_act = pre_act + lax.dot_general(
                    block,
                    weights[tap_t, tap_h, tap_w],
                    (((1,), (1,)), ((), ())),
                    preferred_element_type=F32,
                )
    sigma = jax.nn.sigmoid(pre_act)
    decoded = (pre_act * sigma).astype(BF).reshape(frames.shape)
    scaled = (
        cotangent.reshape(-1, channels).astype(F32) * sigma * (1.0 + pre_act * (1.0 - sigma))
    ).astype(BF)
    own = lax.dot_general(order, scaled, (((1,), (1,)), ((), ())), preferred_element_type=F32)
    own, *far = lax.optimization_barrier((own.astype(BF).reshape(4, 96, -1), *far))
    both = across(jnp.concatenate([own, own]), ("co", "y"))
    line = [rows, *near, jnp.concatenate(far, 2)]
    line_peer = jnp.stack([jnp.where(core == 0, v[1:3], v[0:2]) for v in line])
    line_peer = exchanged(line_peer, "co", 1)
    scaled_rows = scaled.reshape(frames.shape)
    above = shifted(scaled_rows[:, -1:], HEIGHT, 1)
    below = shifted(scaled_rows[:, :1], HEIGHT, -1)
    where = jnp.stack([core, lax.axis_index("y")])
    parts = weight_grad(where, both, line, line_peer)
    parts = across(parts, "x")
    mine = reduced_over_ring(jnp.sum(parts.astype(F32), 0))
    theirs = exchanged(mine, "co", 1)
    taps = jnp.where(
        core == 0,
        jnp.concatenate([mine, theirs[1:]], 0),
        jnp.concatenate([theirs, mine[1:]], 0),
    ).astype(F32)
    kernel_grad = taps.reshape(3, 3, 3, 24, channels).transpose(3, 0, 1, 2, 4)

    tall = jnp.concatenate([above, scaled_rows, below], 1)
    left = shifted(tall[:, :, -1:], "z", 1)
    right = shifted(tall[:, :, :1], "z", -1)
    grad_rimmed = jnp.concatenate([left, tall, right], 2)
    head = input_grad(grad_rimmed, weights, 0, 0, 1)
    carried = shifted(head, TM, -1)
    tail = input_grad(grad_rimmed, weights, 2, 1, 0, (carried,))
    cache_grad, frame_grad = head.reshape(frames.shape), tail.reshape(frames.shape)
    return (decoded, frame_grad, cache_grad, kernel_grad)


def solution(mesh):
    split = Mesh(mesh.devices.reshape(2, 2, 4, 4, 4), ("zh", "co", "x", "y", "z"))
    block = P(TM, HEIGHT, "z", None)
    return jax.shard_map(
        program,
        mesh=split,
        in_specs=(block, P(None, HEIGHT, "z", None), P(), P(), block),
        out_specs=(block, block, block, P(HEIGHT, None, None, None, None)),
        check_vma=False,
    )
```

```python
import functools

import jax
import jax.numpy as jnp
from jax import lax
from jax.experimental import pallas as pl
from jax.experimental.pallas import tpu as pltpu
from jax.sharding import Mesh, PartitionSpec as P

BF = jnp.bfloat16
F32 = jnp.float32
TM = ("zh", "co")
HEIGHT = ("x", "y")
RING = ("zh", "z")
N_TAPS = 14


def shifted(value, axis, by):
    length = lax.axis_size(axis)
    pairs = [(i, i + by) for i in range(length) if 0 <= i + by < length]
    return lax.ppermute(value, axis, pairs)


def exchanged(value, axis, flip):
    return lax.ppermute(value, axis, [(i, i ^ flip) for i in range(lax.axis_size(axis))])


def with_halo(value, sides, width):
    for axis, dim in sides:
        size, length = (lax.axis_size(axis), value.shape[dim])
        up = [(i, (i + 1) % size) for i in range(size - 1)]
        down = [(j, i) for i, j in up]
        last = lax.slice_in_dim(value, length - width, length, axis=dim)
        initial = lax.slice_in_dim(value, 0, width, axis=dim)
        before = lax.ppermute(last, axis, up)
        after = lax.ppermute(initial, axis, down)
        value = jnp.concatenate([before, value, after], axis=dim)
    return value


def tap_block(padded, tap_t, tap_h, tap_w, depth_count, row_count, col_count):
    block = padded[
        tap_t : tap_t + depth_count, tap_h : tap_h + row_count, tap_w : tap_w + col_count
    ]
    return block.reshape(-1, block.shape[-1])


def weight_grad_kernel(where_ref, scaled_ref, *refs):
    lines, both_ref, out_ref, cols = refs[:4], refs[4], refs[5], refs[6]
    core = where_ref[0]

    @pl.when(pl.program_id(0) == 0)
    def _():
        for n, flip in enumerate((0, 1, 3, 2)):
            src = where_ref[1] ^ flip
            at = jnp.where(src == 0, 0, 1 + 4 * src)
            for c in range(3):
                for f in range(3):
                    cols[c, f + 2 * core, pl.ds(at, 5)] = lines[n][f, :, c : c + 32, :]
                for f in range(2):
                    cols[c, f + 3 * (1 - core), pl.ds(at, 5)] = both_ref[n, f, :, c : c + 32, :]

    total = None
    taps = [2 * pl.program_id(0) + n + 4 * core for n in range(2)]
    for src in range(8):
        patch = jnp.concatenate(
            [
                cols[k % 3, pl.ds(k // 9 + src // 4 * 2, 2), pl.ds(src % 4 * 4 + k // 3 % 3, 4)]
                .reshape(256, 384)
                for k in taps
            ],
            1,
        )
        term = jnp.dot(scaled_ref[src], patch, preferred_element_type=F32)
        total = term if total is None else total + term
    for n in range(2):
        for q in range(4):
            out_ref[q, n] = total[24 * q : 24 * q + 24, 384 * n : 384 * n + 384].astype(BF)


def weight_grad(where, scaled, lines, both):
    return pl.pallas_call(
        weight_grad_kernel,
        out_shape=jax.ShapeDtypeStruct((4, N_TAPS, 24, 384), BF),
        grid_spec=pltpu.PrefetchScalarGridSpec(
            num_scalar_prefetch=1,
            grid=(N_TAPS // 2,),
            in_specs=[pl.BlockSpec(memory_space=pltpu.VMEM)] * 6,
            out_specs=pl.BlockSpec((4, 2, 24, 384), lambda j, *_: (0, j, 0, 0)),
            scratch_shapes=[pltpu.VMEM((3, 5, 18, 32, 384), BF)],
        ),
        compiler_params=pltpu.CompilerParams(vmem_limit_bytes=16 << 20),
        cost_estimate=pl.CostEstimate(
            flops=2 * N_TAPS * 384 * 384 * 512, bytes_accessed=9 << 20, transcendentals=0
        ),
    )(where, scaled, *lines, both)


def input_grad_kernel(one_frame, one_slot, rim_ref, *refs):
    more, weight_ref, out_ref, cols, total = refs[:-4], refs[-4], refs[-3], refs[-2], refs[-1]
    step = pl.program_id(0)

    @pl.when(step == 0)
    def _():
        total[...] = jnp.zeros_like(total)
        for c in range(3):
            cols[c] = rim_ref[:, :, 2 - c : 34 - c, :]

    rows = pl.ds(2 - step % 3, 4)
    weight = weight_ref[0, 0].reshape(1152, 384)

    @pl.when(step < 3)
    def _():
        block = jnp.concatenate([cols[c, :, rows].reshape(256, 384) for c in range(3)], 1)
        term = jnp.dot(block, weight, preferred_element_type=F32)
        total[...] += term.reshape(2, 128, 384)

    @pl.when(step >= 3)
    def _():
        block = jnp.concatenate([cols[c, one_frame, rows].reshape(128, 384) for c in range(3)], 1)
        total[one_slot] += jnp.dot(block, weight, preferred_element_type=F32)

    @pl.when(step == 5)
    def _():
        result = total[...]
        for ref in more:
            result = result + ref[...].astype(F32)
        out_ref[...] = result.astype(BF)


def input_grad(rimmed, weights, tap_t, one_frame, one_slot, more=()):
    return pl.pallas_call(
        functools.partial(input_grad_kernel, one_frame, one_slot),
        out_shape=jax.ShapeDtypeStruct((2, 128, 384), BF),
        grid=(6,),
        in_specs=[pl.BlockSpec(memory_space=pltpu.VMEM)] * (1 + len(more))
        + [
            pl.BlockSpec(
                (1, 1, 3, 384, 384), lambda j: (jnp.where(j < 3, tap_t, 1), j % 3, 0, 0, 0)
            )
        ],
        out_specs=pl.BlockSpec((2, 128, 384), lambda j: (0, 0, 0)),
        scratch_shapes=[pltpu.VMEM((3, 2, 6, 32, 384), BF), pltpu.VMEM((2, 128, 384), F32)],
        compiler_params=pltpu.CompilerParams(vmem_limit_bytes=60 << 20),
        cost_estimate=pl.CostEstimate(
            flops=27 * 256 * 384 * 384, bytes_accessed=6 << 20, transcendentals=0
        ),
    )(rimmed, *more, weights)


def across(value, axes):
    return lax.all_to_all(value, axes, 0, 0, tiled=True)


def reduced_over_ring(mine):
    chunks = mine.astype(BF).reshape(8, 42, 384)
    got = across(chunks, RING)
    total = jnp.sum(got.astype(F32), 0).astype(BF)
    whole = across(jnp.broadcast_to(total, chunks.shape), RING)
    return whole.reshape(N_TAPS, 24, 384)


def program(frames, cache_in, kernel, conv_bias, cotangent):
    frame_count, row_count, col_count, channels = frames.shape
    core = lax.axis_index("co")
    is_first = lax.axis_index(TM) == 0
    row = lax.broadcasted_iota(jnp.int32, (2 * channels, channels), 0) % channels
    col = lax.broadcasted_iota(jnp.int32, (2 * channels, channels), 1)
    order = (row // 24 % 4 * 96 + row // 96 * 24 + row % 24 == col).astype(BF)
    order, conv_bias = lax.optimization_barrier((order, conv_bias))
    weights = kernel.transpose(1, 2, 3, 0, 4)
    earlier = shifted(frames, TM, 1)
    earlier = jnp.where(is_first, cache_in, earlier)
    stacked = jnp.concatenate([earlier, frames], 0)
    extended = with_halo(stacked, ((HEIGHT, 1), ("z", 2)), 1)
    rows = lax.dynamic_slice(
        extended,
        (core, (lax.axis_index("y") != 0).astype(jnp.int32), 0, 0),
        (3, 5, col_count + 2, channels),
    )
    rows = jnp.pad(rows, ((0, 0), (0, 0), (0, 6), (0, 0)))
    near = [exchanged(rows, "y", flip) for flip in (1, 3)]
    pre_act = jnp.zeros((frame_count * row_count * col_count, channels), F32) + conv_bias
    for tap_t in range(3):
        for tap_h in range(3):
            if tap_t == 2 and tap_h == 2:
                pre_act, *near = lax.optimization_barrier((pre_act, *near))
                far = [exchanged(near[0][:, :, :16], "y", 3), exchanged(near[1][:, :, 16:], "y", 1)]
            for tap_w in range(3):
                block = tap_block(extended, tap_t, tap_h, tap_w, frame_count, row_count, col_count)
                pre_act = pre_act + lax.dot_general(
                    block,
                    weights[tap_t, tap_h, tap_w],
                    (((1,), (1,)), ((), ())),
                    preferred_element_type=F32,
                )
    sigma = jax.nn.sigmoid(pre_act)
    decoded = (pre_act * sigma).astype(BF).reshape(frames.shape)
    scaled = (
        cotangent.reshape(-1, channels).astype(F32) * sigma * (1.0 + pre_act * (1.0 - sigma))
    ).astype(BF)
    own = lax.dot_general(order, scaled, (((1,), (1,)), ((), ())), preferred_element_type=F32)
    both = across(own.astype(BF).reshape(8, 96, -1), ("co", "y"))
    line = [rows, *near, jnp.concatenate(far, 2)]
    line_peer = jnp.stack([jnp.where(core == 0, v[1:3], v[0:2]) for v in line])
    line_peer = exchanged(line_peer, "co", 1)
    scaled_rows = scaled.reshape(frames.shape)
    above = shifted(scaled_rows[:, -1:], HEIGHT, 1)
    below = shifted(scaled_rows[:, :1], HEIGHT, -1)
    where = jnp.stack([core, lax.axis_index("y")])
    parts = weight_grad(where, both, line, line_peer)
    parts = across(parts, "x")
    mine = reduced_over_ring(jnp.sum(parts.astype(F32), 0))
    theirs = exchanged(mine, "co", 1)
    taps = jnp.where(
        core == 0,
        jnp.concatenate([mine, theirs[1:]], 0),
        jnp.concatenate([theirs, mine[1:]], 0),
    ).astype(F32)
    kernel_grad = taps.reshape(3, 3, 3, 24, channels).transpose(3, 0, 1, 2, 4)

    tall = jnp.concatenate([above, scaled_rows, below], 1)
    left = shifted(tall[:, :, -1:], "z", 1)
    right = shifted(tall[:, :, :1], "z", -1)
    grad_rimmed = jnp.concatenate([left, tall, right], 2)
    head = input_grad(grad_rimmed, weights, 0, 0, 1)
    carried = shifted(head, TM, -1)
    tail = input_grad(grad_rimmed, weights, 2, 1, 0, (carried,))
    cache_grad, frame_grad = head.reshape(frames.shape), tail.reshape(frames.shape)
    return (decoded, frame_grad, cache_grad, kernel_grad)


def solution(mesh):
    split = Mesh(mesh.devices.reshape(2, 2, 4, 4, 4), ("zh", "co", "x", "y", "z"))
    block = P(TM, HEIGHT, "z", None)
    return jax.shard_map(
        program,
        mesh=split,
        in_specs=(block, P(None, HEIGHT, "z", None), P(), P(), block),
        out_specs=(block, block, block, P(HEIGHT, None, None, None, None)),
        check_vma=False,
    )
```
